32 devices in a mesh: dp: 4 (over z), expert: 8 (over y, x, core).
Axes of the slice: x: 2, y: 2, z: 4, core: 2. Of those that a mesh axis runs over, the one named last changes fastest.
Arguments:
- tokens: bfloat16 [4096, 2048], P(('dp', 'expert')), may hold values from -6 to 6
- lengths: int32 [32], P(('dp', 'expert')), may hold values from 1 to 128, 2944 in all
- routes: int32 [4096, 4], P(('dp', 'expert')), may hold values from 0 to 7, all different within a row; in each aligned block of 128 rows (0 to 127, 128 to 255, ...) at most 80 rows name the same one
- gate_values: float32 [4096, 4], P(('dp', 'expert')), may hold values from 0.15 to 0.45
- cotangent: bfloat16 [4096, 2048], P(('dp', 'expert')), may hold values from -6 to 6
- norm1_gain: bfloat16 [2048], P(('dp', 'expert')), may hold values from 0.5 to 1.5
- qkv_weight: bfloat16 [2048, 6144], P(('dp', 'expert')), may hold values from -0.125 to 0.125
- qkv_bias: bfloat16 [6144], P(('dp', 'expert')), may hold values from -2 to 2
- out_weight: bfloat16 [2048, 2048], P(('dp', 'expert')), may hold values from -0.5 to 0.5
- norm2_gain: bfloat16 [2048], P(('dp', 'expert')), may hold values from 0.5 to 1.5
- shared_in: bfloat16 [2048, 2, 5632], P(None, None, ('dp', 'expert')), may hold values from -0.125 to 0.125
- shared_out: bfloat16 [5632, 2048], P(('dp', 'expert')), may hold values from -0.15625 to 0.15625
- shared_gate: bfloat16 [2048], P(('dp', 'expert')), may hold values from -0.125 to 0.125
- expert_in: bfloat16 [8, 2048, 2816], P('expert'), may hold values from -0.125 to 0.125
- expert_out: bfloat16 [8, 1408, 2048], P('expert'), may hold values from -0.21875 to 0.21875
Outputs:
- output: bfloat16 [4096, 2048], P(('dp', 'expert'))
- tokens_grad: float32 [4096, 2048], P(('dp', 'expert'))
- norm1_grad: float32 [2048], P(('dp', 'expert'))
- qkv_weight_grad: float32 [2048, 6144], P(('dp', 'expert'))
- qkv_bias_grad: float32 [6144], P(('dp', 'expert'))
- out_weight_grad: float32 [2048, 2048], P(('dp', 'expert'))
- norm2_grad: float32 [2048], P(('dp', 'expert'))
- shared_in_grad: float32 [2048, 2, 5632], P(None, None, ('dp', 'expert'))
- shared_out_grad: float32 [5632, 2048], P(('dp', 'expert'))
- shared_gate_grad: float32 [2048], P(('dp', 'expert'))
- expert_in_grad: float32 [8, 2048, 2816], P('expert', 'dp')
- expert_out_grad: float32 [8, 1408, 2048], P('expert', 'dp')
- gate_values_grad: float32 [4096, 4], P(('dp', 'expert'))
The draws below stay inside these ranges and needn't reach their ends.
Inputs may be any that keep to these rules, and one draw needn't show every extreme that they name: `routes`: each row names 4 different experts; among the 128 rows of one device no expert is named more than 80 times, a bound that some block reaches. The lengths sum to 2944; the largest is 128.
All inputs are finite; a program needn't handle non-finite values. No bound on the sum of `lengths` on one device may be relied on, other than what follows from the above.
Results may differ from the reference program's by a relative error of at most 0.015.
Values may be sent and summed in bfloat16 or wider, within the bound.
No kernel may reach another device: no remote copies, remote signals or barrier semaphores. Data moves between devices by JAX's collectives and lax.ppermute only.
A program may use at most 320 MiB of HBM per device.

```python
import math
import jax
import jax.numpy as jnp
import numpy as np
from jax import lax

D = 2048
HEADS = 16
HEAD = 128
FFE = 1408
FFS = 5632
TOP = 4
TOK_DEV = 128
SEQS = 32
TOKENS = 4096
EXPERTS = 8
VALID = 2944
CAP = 460
MOST = 80
N_DP = 4


def levels(rng, shape, shards, least, top_value):
    def one(dim, blocks):
        steps = jax.random.uniform(jax.random.fold_in(jax.random.fold_in(rng, 6), dim), (blocks,), jnp.float32, least / len(shards), top_value / len(shards))
        return jnp.repeat(jnp.exp(steps), shape[dim] // blocks).reshape((-1,) + (1,) * (len(shape) - dim - 1))

    loudness = one(*shards[0])
    for cut in shards[1:]:
        loudness = loudness * one(*cut)
    return loudness


def length_profile(number_of, total, limit, lean):
    weights = [(1 << 20) // math.isqrt(rank ** lean) + 1 for rank in range(2, number_of + 1)]
    spare, counts = total - limit - (number_of - 1), [1] * (number_of - 1)
    while spare > 0:
        free = [i for i in range(number_of - 1) if counts[i] < limit]
        pool, budget = sum([weights[i] for i in free]), spare
        for i in free:
            more = min(limit - counts[i], max(1, budget * weights[i] // pool), spare)
            counts[i] = counts[i] + more
            spare = spare - more
    return np.array([limit] + counts)


def uneven(rng, number_of, total, most, lean):
    if number_of == 2:
        one = jax.random.randint(rng, (), max(1, total - most), min(most, total - 1) + 1)
        return jnp.stack([one, total - one])
    tallies = jnp.asarray(length_profile(number_of, total, most, lean), jnp.int32)
    pairs = (number_of - 1) // 2
    giver, taker = tallies[1:1 + 2 * pairs:2], tallies[2:2 + 2 * pairs:2]
    slack = jnp.minimum(giver - 1, most - taker)
    passed = jax.random.randint(jax.random.fold_in(rng, 1), (pairs,), 0, 1 << 20) % (slack + 1)
    tallies = tallies.at[1:1 + 2 * pairs:2].set(giver - passed).at[2:2 + 2 * pairs:2].set(taker + passed)
    return tallies[jax.random.permutation(jax.random.fold_in(rng, 2), number_of)]


def routed_block(own_key, own, number, rows, amount, top, most, lean):
    order = jax.random.permutation(own_key, amount)
    heavy_load, usual = portions_of(amount, rows * top, most, lean, True), portions_of(amount, rows * top, most, lean, False)
    places = jnp.arange(amount)

    def named(sizes, offset_by):
        used = int((sizes > 0).sum())
        fixed = max(1, used // 4)
        shifted = fixed + (places - fixed + offset_by * (used - fixed)) % max(1, amount - fixed)
        return jnp.zeros((amount,), jnp.int32).at[order[jnp.where(places < fixed, places, shifted)]].set(jnp.asarray(sizes, jnp.int32))

    sizes = jnp.where(number % 4 == 0, named(heavy_load, number // 4), named(usual, number - number // 4 - 1))
    mixed = jax.random.permutation(jax.random.fold_in(own, 3), amount)
    giver, receiver = mixed[0:amount // 2 * 2:2], mixed[1:amount // 2 * 2:2]
    margin = jnp.minimum(sizes[giver] - 1, most - sizes[receiver]) // 2
    margin = jnp.where((giver == order[0]) | (receiver == order[0]) | (sizes[receiver] == 0), 0, jnp.maximum(margin, 0))
    shifted = jax.random.randint(jax.random.fold_in(own, 4), (amount // 2,), 0, 1 << 20) % (margin + 1)
    sizes = sizes.at[giver].add(-shifted).at[receiver].add(shifted)
    labels = jnp.searchsorted(jnp.cumsum(sizes), jnp.arange(rows * top), side="right").astype(jnp.int32)
    listing = labels.reshape(top, rows).T
    listing = listing[jax.random.permutation(jax.random.fold_in(own, 1), rows)]
    offset_by = jax.random.randint(jax.random.fold_in(own, 2), (rows, 1), 0, top)
    return jnp.take_along_axis(listing, (jnp.arange(top)[None, :] + offset_by) % top, axis=1)


def portions_of(amount, total, limit, slope, full):
    loads = [(1 << 20) // math.isqrt(grade ** slope) + 1 for grade in range(1, amount + 1)]
    largest = limit if full else min(limit, max(-(-total // amount), total * loads[0] // sum(loads)))
    least = 1 if total - largest >= amount - 1 else 0
    given, rest = [largest] + [least] * (amount - 1), total - largest - least * (amount - 1)
    while rest > 0:
        candidates = [i for i in range(1, amount) if given[i] < largest] or [i for i in range(1, amount) if given[i] < limit]
        mass, budget = sum([loads[i] for i in candidates]), rest
        for i in candidates:
            more = min(limit - given[i], max(1, budget * loads[i] // mass), rest)
            given[i] = given[i] + more
            rest = rest - more
    return np.array(given)


def normal_values(own_key, shape, deviation, most, pieces=(), kind=jnp.bfloat16):
    gain = levels(own_key, shape, pieces, -0.22, 0.18) if pieces else 1.0
    drawn = jax.random.normal(own_key, shape, jnp.float32) * deviation * gain
    return jnp.minimum(jnp.maximum(drawn, -most), most).astype(kind)


def setup_inputs(seed: int = 0) -> dict:
    key_list = jax.random.split(jax.random.key(seed), 16)
    tokens = normal_values(key_list[0], (TOKENS, D), 1.0, 6.0, ((0, 32),))
    lengths = uneven(key_list[1], SEQS, VALID, TOK_DEV, 1).astype(jnp.int32)
    routes_keys = jax.random.split(jax.random.fold_in(key_list[2], 1), TOKENS // TOK_DEV)
    routes_turns = jax.random.permutation(jax.random.fold_in(key_list[2], 3), TOKENS // TOK_DEV)
    routes = jax.vmap(lambda own, number: routed_block(jax.random.fold_in(key_list[2], 2), own, number, TOK_DEV, EXPERTS, TOP, MOST, 2))(routes_keys, routes_turns).reshape((TOKENS, TOP))
    gate_values = jnp.clip(0.15 + 0.29999998 * jax.random.uniform(key_list[3], (TOKENS, TOP), jnp.float32) ** levels(key_list[3], (TOKENS, TOP), ((0, 32),), -0.2, 0.2), 0.15, 0.45)
    cotangent = normal_values(key_list[4], (TOKENS, D), 1.0, 6.0, ((0, 32),))
    norm1_gain = jnp.clip(1.0 + 0.1 * jax.random.normal(key_list[5], (D,), jnp.float32), 0.5, 1.5).astype(jnp.bfloat16)
    qkv_weight = normal_values(key_list[6], (D, 3 * D), D ** -0.5, 0.125, ((0, 32),))
    qkv_bias = normal_values(key_list[7], (3 * D,), 0.3, 2.0, ((0, 32),))
    out_weight = normal_values(key_list[8], (D, D), (D // 16) ** -0.5, 0.5, ((0, 32),))
    norm2_gain = jnp.clip(1.0 + 0.1 * jax.random.normal(key_list[9], (D,), jnp.float32), 0.5, 1.5).astype(jnp.bfloat16)
    shared_in = normal_values(key_list[10], (D, 2, FFS), D ** -0.5, 0.125, ((2, 32),))
    shared_out = normal_values(key_list[11], (FFS, D), (FFS // 4) ** -0.5, 0.15625, ((0, 32),))
    shared_gate = normal_values(key_list[12], (D,), D ** -0.5, 0.125, ((0, 32),))
    expert_in = normal_values(key_list[13], (EXPERTS, D, 2 * FFE), D ** -0.5, 0.125, ((0, 8),))
    expert_out = normal_values(key_list[14], (EXPERTS, FFE, D), (FFE // 2) ** -0.5, 0.21875, ((0, 8),))
    return {"tokens": tokens, "lengths": lengths, "routes": routes, "gate_values": gate_values, "cotangent": cotangent, "norm1_gain": norm1_gain, "qkv_weight": qkv_weight, "qkv_bias": qkv_bias, "out_weight": out_weight, "norm2_gain": norm2_gain, "shared_in": shared_in, "shared_out": shared_out, "shared_gate": shared_gate, "expert_in": expert_in, "expert_out": expert_out}


NORM_EPS = 1e-06
THETA = 1000000.0
HIGH = lax.Precision.HIGHEST

@jax.custom_vjp
def low(v):
    return lax.optimization_barrier(v.astype(jnp.bfloat16)).astype(jnp.float32)

@jax.custom_vjp
def low_back(v):
    return v

def low_keep(v):
    return (low(v), None)

def low_pass(kept, grad):
    return (grad,)

def back_keep(v):
    return (v, None)

def back_low(kept, grad):
    return (low(grad),)
low.defvjp(low_keep, low_pass)
low_back.defvjp(back_keep, back_low)

def rms_scale(inputs, gain_vec):
    return inputs * lax.rsqrt(lax.optimization_barrier(jnp.mean(inputs * inputs, axis=-1, keepdims=True)) + NORM_EPS) * gain_vec

def rotary_tables(row_count, head_width):
    half_width = head_width // 2
    freqs = THETA ** (-(jnp.arange(half_width, dtype=jnp.float32) * 2.0) / head_width)
    angles = jnp.arange(row_count, dtype=jnp.float32)[:, None] * freqs[None, :]
    return (jnp.cos(angles), jnp.sin(angles))

def rotate(inputs, cos_table, sin_table):
    half_width = inputs.shape[-1] // 2
    first = inputs[..., :half_width]
    second = inputs[..., half_width:]
    cos_part = cos_table[:, None, :]
    sin_part = sin_table[:, None, :]
    return jnp.concatenate([first * cos_part - second * sin_part, second * cos_part + first * sin_part], axis=-1)

def swiglu(joined):
    half_width = joined.shape[-1] // 2
    return jax.nn.silu(joined[..., :half_width]) * joined[..., half_width:]

def attend(operands):
    query_heads, key_heads, value_heads = operands
    row_count = query_heads.shape[0]
    scores = jnp.einsum('qhd,khd->hqk', query_heads, key_heads, precision=HIGH) * (1.0 / math.sqrt(HEAD))
    scores = low_back(scores)
    positions = jnp.arange(row_count, dtype=jnp.int32)
    causal = positions[:, None] >= positions[None, :]
    scores = jnp.where(causal[None, :, :], scores, -1e+30)
    attn_probs = jax.nn.softmax(scores, axis=-1)
    return jnp.einsum('hqk,khd->qhd', low(attn_probs), value_heads, precision=HIGH)

def expert_apply(operands):
    block_rows, weight_in, weight_out = operands
    expert_pre = low_back(jnp.dot(block_rows, weight_in, precision=HIGH))
    expert_act = low(swiglu(expert_pre))
    return low_back(low(jnp.dot(expert_act, weight_out, precision=HIGH)))

def reference(tokens, lengths, routes, gate_values, cotangent, norm1_gain, qkv_weight, qkv_bias, out_weight, norm2_gain, shared_in, shared_out, shared_gate, expert_in, expert_out):
    position = jnp.arange(TOKENS, dtype=jnp.int32) % TOK_DEV
    sequence = jnp.arange(TOKENS, dtype=jnp.int32) // TOK_DEV
    valid_tok = position < jnp.take(lengths, sequence)
    pair_live = jnp.broadcast_to(valid_tok[:, None], (TOKENS, TOP)).reshape(N_DP, -1)
    chosen = routes.reshape(N_DP, -1)
    onehot = ((chosen[:, :, None] == jnp.arange(EXPERTS, dtype=jnp.int32)[None, None, :]) & pair_live[:, :, None]).astype(jnp.int32)
    earlier = (jnp.cumsum(onehot, axis=1) - onehot).astype(jnp.int32)
    slot_rank = lax.optimization_barrier(jnp.sum(earlier * onehot, axis=2)).astype(jnp.int32)
    pair_kept = pair_live & (slot_rank < CAP)
    group_ids = jnp.arange(N_DP, dtype=jnp.int32)[:, None]
    slot_total = N_DP * EXPERTS * CAP
    flat_index = jnp.where(pair_kept, (group_ids * EXPERTS + chosen) * CAP + slot_rank, slot_total).reshape(-1).astype(jnp.int32)
    pair_token = jnp.arange(TOKENS * TOP, dtype=jnp.int32) // TOP
    slot_token = jnp.zeros((slot_total,), jnp.int32).at[flat_index].set(pair_token, mode='drop')
    slot_live = jnp.zeros((slot_total,), jnp.float32).at[flat_index].set(1.0, mode='drop')
    pair_slot = jnp.minimum(flat_index, slot_total - 1).astype(jnp.int32)
    kept_float = pair_kept.reshape(TOKENS, TOP).astype(jnp.float32)
    valid_float = valid_tok.astype(jnp.float32)[:, None]
    cos_table, sin_table = rotary_tables(TOK_DEV, HEAD)
    head_shape = (SEQS, TOK_DEV, HEADS, HEAD)

    def forward(token_rows, gate_rows, norm1_full, qkv_full, bias_full, out_full, norm2_full, shared_in_full, shared_out_full, shared_gate_full, expert_in_full, expert_out_full):
        normed1 = low(rms_scale(token_rows, norm1_full))
        qkv_lin = low_back(jnp.dot(normed1, qkv_full, precision=HIGH) + bias_full)
        query_heads = low(rotate(qkv_lin[:, :D].reshape(head_shape), cos_table, sin_table))
        key_heads = low(rotate(qkv_lin[:, D:2 * D].reshape(head_shape), cos_table, sin_table))
        value_heads = low(qkv_lin[:, 2 * D:].reshape(head_shape))
        mixed_rows = lax.map(jax.checkpoint(attend), (query_heads, key_heads, value_heads))
        mixed_rows = low_back(low(mixed_rows.reshape(TOKENS, D)))
        hidden = token_rows + low_back(jnp.dot(mixed_rows, out_full, precision=HIGH))
        normed2 = low(rms_scale(hidden, norm2_full))
        shared_pre = low_back(jnp.dot(normed2, shared_in_full.reshape(D, 2 * FFS), precision=HIGH))
        shared_act = low(swiglu(shared_pre))
        shared_val = low_back(jnp.dot(shared_act, shared_out_full, precision=HIGH))
        shared_weight = jax.nn.sigmoid(jnp.dot(normed2, shared_gate_full, precision=HIGH))
        expert_rows = low_back(jnp.take(normed2, slot_token, axis=0) * slot_live[:, None])
        expert_rows = expert_rows.reshape(N_DP, EXPERTS, CAP, D).transpose(1, 0, 2, 3).reshape(EXPERTS, N_DP * CAP, D)
        produced = lax.map(jax.checkpoint(expert_apply), (expert_rows, expert_in_full, expert_out_full))
        produced = produced.reshape(EXPERTS, N_DP, CAP, D).transpose(1, 0, 2, 3).reshape(slot_total, D)
        picked = jnp.take(produced, pair_slot, axis=0).reshape(TOKENS, TOP, D)
        routed = lax.optimization_barrier(jnp.sum(picked * (gate_rows * kept_float)[:, :, None], axis=1))
        return valid_float * (hidden + shared_weight[:, None] * shared_val + routed)
    primal_args = (tokens.astype(jnp.float32), gate_values, norm1_gain.astype(jnp.float32), qkv_weight.astype(jnp.float32), qkv_bias.astype(jnp.float32), out_weight.astype(jnp.float32), norm2_gain.astype(jnp.float32), shared_in.astype(jnp.float32), shared_out.astype(jnp.float32), shared_gate.astype(jnp.float32), expert_in.astype(jnp.float32), expert_out.astype(jnp.float32))
    output, pullback = jax.vjp(forward, *primal_args)
    gradients = pullback(cotangent.astype(jnp.float32))
    return (output.astype(jnp.bfloat16), gradients[0], gradients[2], gradients[3], gradients[4], gradients[5], gradients[6], gradients[7], gradients[8], gradients[9], gradients[10], gradients[11], gradients[1])
```

```python
import math

import jax
import jax.numpy as jnp
from jax import lax
from jax.sharding import PartitionSpec as P

HEAD = 128
NORM_EPS = 1e-06
THETA = 1000000.0
F32 = jnp.float32
BF16 = jnp.bfloat16


def dot(a, b, dims):
    return lax.dot_general(a, b, (dims, ((), ())), preferred_element_type=F32)


def mm(a, b):
    return dot(a, b, ((1,), (0,)))


def mm_nt(a, b):
    return dot(a, b, ((1,), (1,)))


def mm_tn(a, b):
    return dot(a, b, ((0,), (0,)))


def plane_masks(size, me):
    if size == 8:
        even = jnp.array([0, 2, 4, 6, 1, 5, 3, 7], jnp.int32)
        odd = jnp.array([0, 4, 2, 6, 1, 3, 5, 7], jnp.int32)
        return jnp.where(me % 2 == 0, even, odd)
    return jnp.arange(size, dtype=jnp.int32)


def first_hop(i):
    return i ^ 2 if i % 2 == 0 else i ^ 4


def second_hop(i):
    return i ^ 4 if i % 2 == 0 else i ^ 2


def send(block, size, target):
    return lax.ppermute(block, "expert", [(i, target(i)) for i in range(size)])


def core_swap(i):
    return i ^ 1


def plane_gather(block, size):
    if size == 8:
        one = send(block, size, first_hop)
        two = send(block, size, second_hop)
        three = send(one, size, second_hop)
        near = [block, one, two, three]
        return near + [send(part, size, core_swap) for part in near]
    return [block] + [send(block, size, lambda i, m=m: i ^ m) for m in range(1, size)]


def plane_sum(parts, size):
    if size == 8:
        low = parts.astype(BF16)
        got = send(low[4:], size, core_swap)
        near = parts[:4] + got.astype(F32)
        got = send(near[2:].astype(BF16), size, second_hop)
        near = near[:2] + got.astype(F32)
        got = send(near[1].astype(BF16), size, first_hop)
        return near[0] + got.astype(F32)
    low = parts.astype(BF16)
    total = parts[0]
    for m in range(1, size):
        total = total + send(low[m], size, lambda i, m=m: i ^ m).astype(F32)
    return total


def norm_scale(rows):
    return lax.rsqrt(jnp.mean(rows * rows, axis=-1, keepdims=True) + NORM_EPS)


def norm_back(rows, scale, gain, grad):
    unit = rows * scale
    weighted = grad * gain
    inner = jnp.mean(weighted * unit, axis=-1, keepdims=True)
    return scale * (weighted - unit * inner), jnp.sum(grad * unit, axis=0)


def swiglu_parts(gate, up):
    sig = jax.nn.sigmoid(gate)
    return sig, gate * sig * up


def swiglu_back(gate, up, grad):
    sig = jax.nn.sigmoid(gate)
    silu = gate * sig
    return grad * up * (sig + silu * (1.0 - sig)), grad * silu


def rotary_tables(row_count, head_width):
    half_width = head_width // 2
    freqs = THETA ** (-(jnp.arange(half_width, dtype=F32) * 2.0) / head_width)
    angles = jnp.arange(row_count, dtype=F32)[:, None] * freqs[None, :]
    return (jnp.cos(angles), jnp.sin(angles))


def rotate(inputs, cos_table, sin_table):
    half = inputs.shape[-1] // 2
    first, second = inputs[..., :half], inputs[..., half:]
    cos_part, sin_part = cos_table[None, :, None, :], sin_table[None, :, None, :]
    return jnp.concatenate(
        [first * cos_part - second * sin_part, second * cos_part + first * sin_part], axis=-1
    )


def shards(
    tokens,
    lengths,
    routes,
    gate_values,
    cotangent,
    norm1_gain,
    qkv_weight,
    qkv_bias,
    out_weight,
    norm2_gain,
    shared_in,
    shared_out,
    shared_gate,
    expert_in,
    expert_out,
):
    rows, width = tokens.shape
    top = routes.shape[1]
    group = lax.axis_size("expert")
    planes = lax.axis_size("dp")
    devices = group * planes
    both = ("dp", "expert")
    me = lax.axis_index("expert")
    plane = lax.axis_index("dp")
    heads = width // HEAD
    own_heads = heads // group
    shard = qkv_weight.shape[0]
    split = HEAD // shard
    lanes = group // split
    experts = group * expert_in.shape[0]
    valid_total = 23 * rows * devices // 32
    capacity = 5 * valid_total * top // (4 * experts * planes)
    slots = -(-capacity // 16) * 16
    order = me ^ plane_masks(group, me)
    group_rows = group * rows

    vectors = jnp.concatenate([norm1_gain, norm2_gain, shared_gate, qkv_bias]).astype(F32)
    vector_rows = -(-vectors.shape[0] // 128)
    vectors = jnp.pad(vectors, (0, vector_rows * 128 - vectors.shape[0])).reshape(vector_rows, 128)
    info = jnp.concatenate(
        [
            vectors,
            routes.T.astype(F32),
            gate_values.T,
            jnp.broadcast_to(lengths.astype(F32)[:, None], (1, rows)),
        ],
        axis=0,
    )
    told = lax.all_to_all(
        jnp.broadcast_to(info[None], (devices,) + info.shape), both, 0, 0, tiled=True
    )
    flat = told[:, :vector_rows].reshape(devices, vector_rows * 128)
    norm1_full = flat[:, :shard].reshape(width)
    norm2_full = flat[:, shard : 2 * shard].reshape(width)
    gate_full = flat[:, 2 * shard : 3 * shard].reshape(width)
    bias_full = flat[:, 3 * shard : 3 * shard + qkv_bias.shape[0]].reshape(
        3, split, own_heads, lanes, HEAD
    )
    rest = told[:, vector_rows:].reshape(planes, group, 2 * top + 1, rows)
    mine = lax.dynamic_index_in_dim(rest, plane, 0, keepdims=False)
    column = lax.dynamic_index_in_dim(rest, me, 1, keepdims=False)
    slot = jnp.arange(rows, dtype=F32)
    group_routes = mine[:, :top].astype(jnp.int32)
    group_gates = mine[:, top : 2 * top]
    group_valid = slot[None, :] < mine[:, 2 * top]
    column_valid = (slot[None, :] < column[:, 2 * top]).astype(F32).reshape(planes * rows, 1)
    valid_float = (slot < lengths.astype(F32)[0]).astype(F32)[:, None]

    lane, part = me // split, me % split
    by_head = qkv_weight.reshape(shard, 3, split, own_heads, lanes, HEAD)
    by_head = by_head.transpose(4, 2, 0, 1, 3, 5).reshape(group, shard, 3 * own_heads * HEAD)
    by_head = lax.all_to_all(by_head, "expert", 0, 0, tiled=True)
    qkv_own = lax.all_gather(by_head, "dp", axis=0, tiled=True).reshape(width, 3 * own_heads * HEAD)
    bias_own = lax.dynamic_index_in_dim(bias_full, part, 1, keepdims=False)
    bias_own = lax.dynamic_index_in_dim(bias_own, lane, 2, keepdims=False).reshape(-1)
    out_parts = lax.all_gather(out_weight[None], "dp", axis=0, tiled=True)
    pairs = [[k * split + p for p in range(split)] for k in range(lanes)]
    out_own = lax.all_to_all(
        out_parts.reshape(split, own_heads, shard, width),
        "expert",
        0,
        0,
        axis_index_groups=pairs,
        tiled=True,
    )
    out_own = out_own.transpose(1, 0, 2, 3).reshape(own_heads * HEAD, width)

    group_tokens = jnp.concatenate(plane_gather(tokens, group), axis=0).astype(F32)
    normed1 = (group_tokens * norm_scale(group_tokens) * norm1_full).astype(BF16)
    qkv_lin = mm(normed1, qkv_own) + bias_own
    own_width = own_heads * HEAD
    cos_table, sin_table = rotary_tables(rows, HEAD)
    head_shape = (group, rows, own_heads, HEAD)
    query = rotate(qkv_lin[:, :own_width].reshape(head_shape), cos_table, sin_table).astype(BF16)
    key = rotate(qkv_lin[:, own_width : 2 * own_width].reshape(head_shape), cos_table, sin_table)
    key = key.astype(BF16)
    value = qkv_lin[:, 2 * own_width :].reshape(head_shape).astype(BF16)
    score_scale = 1.0 / math.sqrt(HEAD)
    positions = jnp.arange(rows, dtype=jnp.int32)
    causal = (positions[:, None] >= positions[None, :])[None, None]

    def probs_of(query, key):
        scores = jnp.einsum("sqhd,skhd->shqk", query, key, preferred_element_type=F32)
        scores = jnp.where(causal, scores * score_scale, -1e30)
        peak = jnp.max(scores, axis=-1, keepdims=True)
        raised = jnp.exp(scores - peak)
        return raised / jnp.sum(raised, axis=-1, keepdims=True)

    probs = probs_of(query, key)
    mixed = jnp.einsum("shqk,skhd->sqhd", probs.astype(BF16), value, preferred_element_type=F32)
    mixed = mixed.reshape(group_rows, own_width).astype(BF16)
    branch = plane_sum(mm(mixed, out_own).reshape(group, rows, width), group)
    hidden = tokens.astype(F32) + branch
    scale2 = norm_scale(hidden)
    normed2 = (hidden * scale2 * norm2_full).astype(BF16)
    group_normed = jnp.concatenate(plane_gather(normed2, group), axis=0)
    column_normed = lax.all_gather(normed2, "dp", axis=0, tiled=True)
    group_cot = jnp.concatenate(plane_gather(cotangent, group), axis=0)
    column_cot = lax.all_gather(cotangent, "dp", axis=0, tiled=True)

    named = group_routes == me
    taken = jnp.any(named, axis=1) & group_valid
    gate_here = jnp.sum(jnp.where(named, group_gates, 0.0), axis=1)
    taken_low = taken.astype(BF16)
    before = (positions[:, None] < positions[None, :]).astype(BF16)
    inside = mm(taken_low, before)
    counts = jnp.sum(taken.astype(F32), axis=1)
    places = jnp.arange(group, dtype=jnp.int32)
    offsets = jnp.sum(jnp.where(places[None, :] < places[:, None], counts[None, :], 0.0), axis=1)
    rank = (inside + offsets[:, None]).astype(jnp.int32)
    rank = jnp.where(taken & (rank < capacity), rank, -1)
    rank = jnp.take(rank, order, axis=0).reshape(1, group_rows)
    gate_rel = jnp.take(gate_here, order, axis=0).reshape(1, group_rows)
    chosen = rank == jnp.arange(slots, dtype=jnp.int32)[:, None]
    pick = chosen.astype(BF16)
    row_gate = jnp.sum(jnp.where(chosen, gate_rel, 0.0), axis=1, keepdims=True)
    weight_in, weight_out = expert_in[0], expert_out[0]
    hidden_units = weight_out.shape[0]
    expert_rows = mm(pick, group_normed).astype(BF16)
    cot_rows = mm(pick, group_cot)
    val_grad = (cot_rows * row_gate).astype(BF16)
    expert_pre = mm(expert_rows, weight_in)
    e_gate, e_up = expert_pre[:, :hidden_units], expert_pre[:, hidden_units:]
    expert_act = swiglu_parts(e_gate, e_up)[1].astype(BF16)
    act_grad = mm_nt(val_grad, weight_out)
    out_grad = mm_tn(expert_act, val_grad).astype(BF16)
    expert_out_grad = lax.psum_scatter(out_grad, "dp", scatter_dimension=0, tiled=True)
    pre_grad = jnp.concatenate(swiglu_back(e_gate, e_up, act_grad), axis=1).astype(BF16)
    in_grad = mm_tn(expert_rows, pre_grad).astype(BF16)
    expert_in_grad = lax.psum_scatter(in_grad, "dp", scatter_dimension=0, tiled=True)
    row_grad = mm_nt(pre_grad, weight_in).astype(BF16)
    expert_val = mm(expert_act, weight_out)
    pair_dot = jnp.sum(cot_rows * expert_val, axis=1, keepdims=True)
    routed_part = mm_tn(pick, (expert_val * row_gate).astype(BF16))
    normed_part = mm_tn(pick, row_grad)
    routed_sum = plane_sum(routed_part.reshape(group, rows, width), group)
    routed_grad = plane_sum(normed_part.reshape(group, rows, width), group)
    pair_dots = jnp.sum(jnp.where(chosen, pair_dot, 0.0), axis=0).reshape(group, rows)
    inverse = jnp.argmax(order[None, :] == places[:, None], axis=1)
    pair_dots = jnp.take(pair_dots, inverse, axis=0)
    pair_back = lax.all_to_all(pair_dots, "expert", 0, 0, tiled=True)
    gate_values_grad = jnp.sum(
        jnp.where(routes.T[None] == places[:, None, None], pair_back[:, None, :], 0.0), axis=0
    ).T

    units = shared_out.shape[0]
    unit_in = jnp.concatenate(plane_gather(shared_in.transpose(1, 2, 0), group), axis=1)
    unit_out = jnp.concatenate(plane_gather(shared_out, group), axis=0)
    plane_units = group * units
    shared_weight = jax.nn.sigmoid(
        jnp.sum(column_normed.astype(F32) * gate_full, axis=1, keepdims=True)
    )
    unit_flat = unit_in.reshape(2 * plane_units, width)
    shared_pre = mm_nt(column_normed, unit_flat)
    s_gate, s_up = shared_pre[:, :plane_units], shared_pre[:, plane_units:]
    shared_act = swiglu_parts(s_gate, s_up)[1].astype(BF16)
    shared_val = mm(shared_act, unit_out)
    column_grad = column_cot.astype(F32) * column_valid
    shared_val_grad = (column_grad * shared_weight).astype(BF16)
    logit_grad = jnp.sum(column_grad * shared_val, axis=1, keepdims=True)
    logit_grad = logit_grad * shared_weight * (1.0 - shared_weight)
    gate_grad = jnp.sum(logit_grad * column_normed.astype(F32), axis=0)
    shared_act_grad = mm_nt(shared_val_grad, unit_out)
    shared_pre_grad = jnp.concatenate(swiglu_back(s_gate, s_up, shared_act_grad), axis=1)
    shared_pre_grad = shared_pre_grad.astype(BF16)
    normed_term = mm(shared_pre_grad, unit_flat) + logit_grad * gate_full
    shared_grad = lax.psum_scatter(
        normed_term.astype(BF16), "dp", scatter_dimension=0, tiled=True
    ).astype(F32)
    shared_sum = lax.psum_scatter(
        (shared_weight * shared_val).astype(BF16), "dp", scatter_dimension=0, tiled=True
    ).astype(F32)
    unit_out_grad = mm_tn(shared_act, shared_val_grad)
    unit_in_grad = mm_tn(shared_pre_grad, column_normed)
    shared_out_grad = plane_sum(unit_out_grad.reshape(group, units, width), group)
    unit_in_grad = unit_in_grad.reshape(2, group, units, width).transpose(1, 0, 2, 3)
    shared_in_grad = plane_sum(unit_in_grad, group).transpose(2, 0, 1)

    output = (valid_float * (hidden + shared_sum + routed_sum)).astype(BF16)
    normed2_grad = shared_grad + routed_grad
    norm_term, norm2_part = norm_back(hidden, scale2, norm2_full, normed2_grad)
    hidden_grad = cotangent.astype(F32) * valid_float + norm_term
    branch_grad = jnp.concatenate(plane_gather(hidden_grad.astype(BF16), group), axis=0)

    out_own_grad = mm_tn(mixed, branch_grad).astype(BF16)
    out_own_grad = out_own_grad.reshape(own_heads, split, shard, width).transpose(1, 0, 2, 3)
    out_own_grad = lax.all_to_all(
        out_own_grad, "expert", 0, 0, axis_index_groups=pairs, tiled=True
    ).reshape(planes * shard, width)
    out_weight_grad = lax.psum_scatter(out_own_grad, "dp", scatter_dimension=0, tiled=True)
    mixed_grad = mm_nt(branch_grad, out_own).astype(BF16).reshape(head_shape)
    value_grad = jnp.einsum(
        "shqk,sqhd->skhd", probs.astype(BF16), mixed_grad, preferred_element_type=F32
    )
    probs_grad = jnp.einsum("sqhd,skhd->shqk", mixed_grad, value, preferred_element_type=F32)
    score_grad = probs * (probs_grad - jnp.sum(probs_grad * probs, axis=-1, keepdims=True))
    score_grad = score_grad.astype(BF16)
    query_grad = jnp.einsum("shqk,skhd->sqhd", score_grad, key, preferred_element_type=F32)
    key_grad = jnp.einsum("shqk,sqhd->skhd", score_grad, query, preferred_element_type=F32)
    query_grad = rotate(query_grad * score_scale, cos_table, -sin_table)
    key_grad = rotate(key_grad * score_scale, cos_table, -sin_table)
    flat_shape = (group_rows, own_width)
    qkv_grad = jnp.concatenate(
        [
            query_grad.reshape(flat_shape),
            key_grad.reshape(flat_shape),
            value_grad.reshape(flat_shape),
        ],
        axis=1,
    ).astype(BF16)
    bias_part = jnp.sum(qkv_grad.astype(F32), axis=0)
    normed1_grad = plane_sum(mm_nt(qkv_grad, qkv_own).reshape(group, rows, width), group)
    qkv_own_grad = mm_tn(normed1, qkv_grad).astype(BF16)
    qkv_own_grad = lax.psum_scatter(qkv_own_grad, "dp", scatter_dimension=0, tiled=True)
    qkv_own_grad = lax.all_to_all(
        qkv_own_grad.reshape(group, shard, 3 * own_width), "expert", 0, 0, tiled=True
    )
    qkv_weight_grad = (
        qkv_own_grad.reshape(lanes, split, shard, 3, own_heads, HEAD)
        .transpose(2, 3, 1, 4, 0, 5)
        .reshape(shard, 3 * width)
        .astype(F32)
    )
    own_tokens = tokens.astype(F32)
    token_term, norm1_part = norm_back(own_tokens, norm_scale(own_tokens), norm1_full, normed1_grad)
    tokens_grad = hidden_grad + token_term

    here = (jnp.arange(split)[:, None] == part) & (jnp.arange(lanes)[None, :] == lane)
    bias_all = jnp.where(
        here[None, :, None, :, None], bias_part.reshape(3, 1, own_heads, 1, HEAD), 0.0
    ).reshape(devices, qkv_bias.shape[0])
    sums = jnp.concatenate(
        [
            norm1_part.reshape(devices, shard),
            norm2_part.reshape(devices, shard),
            gate_grad.reshape(devices, shard),
            bias_all,
        ],
        axis=1,
    )
    sums = jnp.pad(sums, ((0, 0), (0, vector_rows * 128 - sums.shape[1])))
    sums = lax.all_to_all(sums.reshape(devices, vector_rows, 128), both, 0, 0, tiled=True)
    sums = jnp.sum(sums, axis=0).reshape(-1)

    return (
        output,
        tokens_grad,
        sums[:shard],
        qkv_weight_grad,
        sums[3 * shard : 3 * shard + qkv_bias.shape[0]],
        out_weight_grad.astype(F32),
        sums[shard : 2 * shard],
        shared_in_grad,
        shared_out_grad,
        sums[2 * shard : 3 * shard],
        expert_in_grad.astype(F32)[None],
        expert_out_grad.astype(F32)[None],
        gate_values_grad,
    )


def solution(mesh):
    both = ("dp", "expert")
    in_specs = (
        P(both, None),
        P(both),
        P(both, None),
        P(both, None),
        P(both, None),
        P(both),
        P(both, None),
        P(both),
        P(both, None),
        P(both),
        P(None, None, both),
        P(both, None),
        P(both),
        P("expert", None, None),
        P("expert", None, None),
    )
    out_specs = (
        P(both, None),
        P(both, None),
        P(both),
        P(both, None),
        P(both),
        P(both, None),
        P(both),
        P(None, None, both),
        P(both, None),
        P(both),
        P("expert", "dp", None),
        P("expert", "dp", None),
        P(both, None),
    )
    return jax.shard_map(shards, mesh=mesh, in_specs=in_specs, out_specs=out_specs, check_vma=False)
```

```python
import math

import jax
import jax.numpy as jnp
import numpy as np
from jax import lax
from jax.sharding import PartitionSpec as P

HEAD = 128
NORM_EPS = 1e-06
THETA = 1000000.0
F32 = jnp.float32
barrier = lax.optimization_barrier
BF16 = jnp.bfloat16


def dot(a, b, dims):
    return lax.dot_general(a, b, (dims, ((), ())), preferred_element_type=F32)


def mm(a, b):
    return dot(a, b, ((1,), (0,)))


def mm_nt(a, b):
    return dot(a, b, ((1,), (1,)))


def mm_tn(a, b):
    return dot(a, b, ((0,), (0,)))


def plane_order(size, me):
    if size == 8:
        even, odd = [0, 2, 4, 6, 1, 5, 3, 7], [0, 4, 2, 6, 1, 3, 5, 7]
        first = me % 2 == 0
        return [me ^ (a if a == b else jnp.where(first, a, b)) for a, b in zip(even, odd)]
    return [me ^ m for m in range(size)]


def first_hop(i):
    return i ^ 2 if i % 2 == 0 else i ^ 4


def second_hop(i):
    return i ^ 4 if i % 2 == 0 else i ^ 2


def send(block, size, target):
    return lax.ppermute(block, "expert", [(i, target(i)) for i in range(size)])


def core_swap(i):
    return i ^ 1


def gather_first(block, size):
    if size == 8:
        return [block, send(block, size, first_hop), send(block, size, second_hop)]
    return [block] + [send(block, size, lambda i, m=m: i ^ m) for m in range(1, size)]


def gather_second(parts, size):
    return parts + [send(parts[1], size, second_hop)] if size == 8 else parts


def gather_third(parts, size):
    return parts + [send(part, size, core_swap) for part in parts] if size == 8 else parts


def plane_gather(block, size):
    return gather_third(gather_second(gather_first(block, size), size), size)


def plane_place(parts, order, whole, place):
    for j, part in enumerate(parts):
        whole = place(whole, part, order[j])
    return whole


def plane_rows(block, size, order):
    rows = block.shape[0]
    whole = jnp.zeros((size * rows,) + block.shape[1:], block.dtype)
    return plane_place(
        plane_gather(block, size),
        order,
        whole,
        lambda whole, part, source: lax.dynamic_update_slice_in_dim(whole, part, source * rows, 0),
    )


def plane_sum(parts, size):
    if size == 8:
        low = parts.astype(BF16)
        got = send(low[4:], size, core_swap)
        near = parts[:4] + got.astype(F32)
        got = send(near[2:].astype(BF16), size, second_hop)
        near = near[:2] + got.astype(F32)
        got = send(near[1].astype(BF16), size, first_hop)
        return near[0] + got.astype(F32)
    low = parts.astype(BF16)
    total = parts[0]
    for m in range(1, size):
        total = total + send(low[m], size, lambda i, m=m: i ^ m).astype(F32)
    return total


def norm_scale(rows):
    return lax.rsqrt(jnp.mean(rows * rows, axis=-1, keepdims=True) + NORM_EPS)


def norm_back(rows, scale, gain, grad):
    unit = rows * scale
    weighted = grad * gain
    inner = jnp.mean(weighted * unit, axis=-1, keepdims=True)
    return scale * (weighted - unit * inner), jnp.sum(grad * unit, axis=0)


def swiglu_parts(gate, up):
    sig = jax.nn.sigmoid(gate)
    return sig, gate * sig * up


def swiglu_back(gate, up, grad):
    sig = jax.nn.sigmoid(gate)
    silu = gate * sig
    return grad * up * (sig + silu * (1.0 - sig)), grad * silu


def rotary_tables(row_count, head_width):
    half_width = head_width // 2
    powers = -(np.arange(half_width, dtype=np.float32) * np.float32(2.0)) / np.float32(head_width)
    freqs = np.power(np.float32(THETA), powers).astype(np.float32)
    angles = np.arange(row_count, dtype=np.float32)[:, None] * freqs[None, :]
    return (jnp.asarray(np.cos(angles)), jnp.asarray(np.sin(angles)))


def rotate(inputs, cos_table, sin_table):
    half = inputs.shape[-1] // 2
    first, second = inputs[..., :half], inputs[..., half:]
    cos_part, sin_part = cos_table[None, :, None, :], sin_table[None, :, None, :]
    return jnp.concatenate(
        [first * cos_part - second * sin_part, second * cos_part + first * sin_part], axis=-1
    )


def shards(
    tokens,
    lengths,
    routes,
    gate_values,
    cotangent,
    norm1_gain,
    qkv_weight,
    qkv_bias,
    out_weight,
    norm2_gain,
    shared_in,
    shared_out,
    shared_gate,
    expert_in,
    expert_out,
):
    rows, width = tokens.shape
    top = routes.shape[1]
    group = lax.axis_size("expert")
    planes = lax.axis_size("dp")
    devices = group * planes
    both = ("dp", "expert")
    me = lax.axis_index("expert")
    plane = lax.axis_index("dp")
    heads = width // HEAD
    own_heads = heads // group
    shard = qkv_weight.shape[0]
    split = HEAD // shard
    lanes = group // split
    experts = group * expert_in.shape[0]
    valid_total = 23 * rows * devices // 32
    capacity = 5 * valid_total * top // (4 * experts * planes)
    slots = -(-capacity // 16) * 16
    order = plane_order(group, me)
    order_list = jnp.stack(order)
    group_rows = group * rows

    vectors = jnp.concatenate([norm1_gain, norm2_gain, shared_gate, qkv_bias]).astype(F32)
    vector_rows = -(-vectors.shape[0] // 128)
    vectors = jnp.pad(vectors, (0, vector_rows * 128 - vectors.shape[0])).reshape(vector_rows, 128)
    info = jnp.concatenate(
        [
            vectors,
            routes.T.astype(F32),
            gate_values.T,
            jnp.broadcast_to(lengths.astype(F32)[:, None], (1, rows)),
        ],
        axis=0,
    )
    lane, part = me // split, me % split
    out_parts = lax.all_gather(out_weight[None], "dp", axis=0, tiled=True)
    by_head = qkv_weight.reshape(shard, 3, split, own_heads, lanes, HEAD)
    by_head = by_head.transpose(4, 2, 0, 1, 3, 5).reshape(group, shard, 3 * own_heads * HEAD)
    by_head = lax.all_to_all(by_head, "expert", 0, 0, tiled=True)
    by_head, token_source, cot_source = barrier((by_head, tokens, cotangent))
    out_parts, info = barrier((out_parts, info))
    qkv_own = lax.all_gather(by_head, "dp", axis=0, tiled=True).reshape(width, 3 * own_heads * HEAD)

    told = lax.all_to_all(
        jnp.broadcast_to(info[None], (devices,) + info.shape), both, 0, 0, tiled=True
    )
    flat = told[:, :vector_rows].reshape(devices, vector_rows * 128)
    norm1_full = flat[:, :shard].reshape(width)
    norm2_full = flat[:, shard : 2 * shard].reshape(width)
    gate_full = flat[:, 2 * shard : 3 * shard].reshape(width)
    bias_full = flat[:, 3 * shard : 3 * shard + qkv_bias.shape[0]].reshape(
        3, split, own_heads, lanes, HEAD
    )
    rest = told[:, vector_rows:].reshape(planes, group, 2 * top + 1, rows)
    mine = lax.dynamic_index_in_dim(rest, plane, 0, keepdims=False)
    column = lax.dynamic_index_in_dim(rest, me, 1, keepdims=False)
    slot = jnp.arange(rows, dtype=F32)
    group_routes = mine[:, :top].astype(jnp.int32)
    group_gates = mine[:, top : 2 * top]
    group_valid = slot[None, :] < mine[:, 2 * top]
    column_valid = (slot[None, :] < column[:, 2 * top]).astype(F32).reshape(planes * rows, 1)
    valid_float = (slot < lengths.astype(F32)[0]).astype(F32)[:, None]

    bias_own = lax.dynamic_index_in_dim(bias_full, part, 1, keepdims=False)
    bias_own = lax.dynamic_index_in_dim(bias_own, lane, 2, keepdims=False).reshape(-1)
    pairs = [[k * split + p for p in range(split)] for k in range(lanes)]
    out_whole = plane_place(
        plane_gather(out_parts.reshape(split, own_heads, shard, width), group),
        order,
        jnp.zeros((lanes, split, own_heads, split, shard, width), BF16),
        lambda whole, block, source: lax.dynamic_update_slice(
            whole, block[None, :, :, None], (source // split, 0, 0, source % split, 0, 0)
        ),
    ).reshape(width, width)
    group_tokens = plane_rows(token_source, group, order).astype(F32)
    group_cot = plane_rows(cot_source, group, order)
    qkv_own, column_source = barrier((qkv_own, cotangent))
    column_cot = lax.all_gather(column_source, "dp", axis=0, tiled=True)

    normed1 = (group_tokens * norm_scale(group_tokens) * norm1_full).astype(BF16)
    qkv_lin = mm(normed1, qkv_own) + bias_own
    own_width = own_heads * HEAD
    cos_table, sin_table = rotary_tables(rows, HEAD)
    places = jnp.arange(group, dtype=jnp.int32)
    head_shape = (group, rows, own_heads, HEAD)
    query = rotate(qkv_lin[:, :own_width].reshape(head_shape), cos_table, sin_table).astype(BF16)
    key = rotate(qkv_lin[:, own_width : 2 * own_width].reshape(head_shape), cos_table, sin_table)
    key = key.astype(BF16)
    value = qkv_lin[:, 2 * own_width :].reshape(head_shape).astype(BF16)
    score_scale = 1.0 / math.sqrt(HEAD)
    positions = jnp.arange(rows, dtype=jnp.int32)
    causal = (positions[:, None] >= positions[None, :])[None, None]

    def probs_of(query, key):
        scores = jnp.einsum("sqhd,skhd->shqk", query, key, preferred_element_type=F32)
        scores = jnp.where(causal, scores * score_scale, -1e30)
        peak = jnp.max(scores, axis=-1, keepdims=True)
        raised = jnp.exp(scores - peak)
        return raised / jnp.sum(raised, axis=-1, keepdims=True)

    probs = probs_of(query, key)
    mixed = jnp.einsum("shqk,skhd->sqhd", probs.astype(BF16), value, preferred_element_type=F32)
    mixed = mixed.reshape(group_rows, own_width).astype(BF16)
    mixed, out_whole, group_cot = barrier((mixed, out_whole, group_cot))
    mixed_parts = gather_first(mixed, group)
    mixed_parts, column_cot = barrier((mixed_parts, column_cot))
    mixed_parts = gather_third(gather_second(mixed_parts, group), group)
    mixed_whole = plane_place(
        mixed_parts,
        order,
        jnp.zeros((group_rows, width), BF16),
        lambda whole, block, source: lax.dynamic_update_slice(whole, block, (0, source * own_width)),
    )
    mixed_whole, unit_in, unit_out = barrier(
        (mixed_whole, shared_in.transpose(1, 2, 0), shared_out)
    )
    unit_in, unit_out = gather_first(unit_in, group), gather_first(unit_out, group)
    group_hidden = group_tokens + mm(mixed_whole, out_whole)
    group_scale2 = norm_scale(group_hidden)
    group_normed = (group_hidden * group_scale2 * norm2_full).astype(BF16)
    hidden = lax.dynamic_slice_in_dim(group_hidden, me * rows, rows, 0)
    scale2 = lax.dynamic_slice_in_dim(group_scale2, me * rows, rows, 0)
    normed2 = lax.dynamic_slice_in_dim(group_normed, me * rows, rows, 0)
    column_normed = lax.all_gather(normed2, "dp", axis=0, tiled=True)

    named = group_routes == me
    taken = jnp.any(named, axis=1) & group_valid
    gate_here = jnp.sum(jnp.where(named, group_gates, 0.0), axis=1)
    taken_low = taken.astype(BF16)
    before = (positions[:, None] < positions[None, :]).astype(BF16)
    inside = mm(taken_low, before)
    counts = jnp.sum(taken.astype(F32), axis=1)
    places = jnp.arange(group, dtype=jnp.int32)
    offsets = jnp.sum(jnp.where(places[None, :] < places[:, None], counts[None, :], 0.0), axis=1)
    rank = (inside + offsets[:, None]).astype(jnp.int32)
    rank = jnp.where(taken & (rank < capacity), rank, -1)
    slot_ids = jnp.arange(slots, dtype=jnp.int32)[:, None]
    chosen = rank.reshape(1, group_rows) == slot_ids
    pick = chosen.astype(BF16)
    put = (jnp.take(rank, order_list, axis=0).reshape(1, group_rows) == slot_ids).astype(BF16)
    row_gate = jnp.sum(
        jnp.where(chosen, gate_here.reshape(1, group_rows), 0.0), axis=1, keepdims=True
    )
    weight_in, weight_out = expert_in[0], expert_out[0]
    hidden_units = weight_out.shape[0]
    expert_rows = mm(pick, group_normed).astype(BF16)
    cot_rows = mm(pick, group_cot)
    val_grad = (cot_rows * row_gate).astype(BF16)
    expert_pre = mm(expert_rows, weight_in)
    expert_pre, unit_in, unit_out = barrier((expert_pre, unit_in, unit_out))
    unit_in, unit_out = gather_second(unit_in, group), gather_second(unit_out, group)
    e_gate, e_up = expert_pre[:, :hidden_units], expert_pre[:, hidden_units:]
    expert_act = swiglu_parts(e_gate, e_up)[1].astype(BF16)
    act_grad = mm_nt(val_grad, weight_out)
    out_grad = mm_tn(expert_act, val_grad).astype(BF16)
    pre_grad = jnp.concatenate(swiglu_back(e_gate, e_up, act_grad), axis=1).astype(BF16)
    in_grad = mm_tn(expert_rows, pre_grad).astype(BF16)
    row_grad = mm_nt(pre_grad, weight_in).astype(BF16)
    expert_val = mm(expert_act, weight_out)
    pair_dot = jnp.sum(cot_rows * expert_val, axis=1, keepdims=True)
    routed_part = mm_tn(put, (expert_val * row_gate).astype(BF16))
    normed_part = mm_tn(put, row_grad)
    routed_sum = plane_sum(routed_part.reshape(group, rows, width), group)
    routed_grad = plane_sum(normed_part.reshape(group, rows, width), group)
    pair_dots = jnp.sum(jnp.where(chosen, pair_dot, 0.0), axis=0).reshape(group, rows)
    pair_back = lax.all_to_all(pair_dots, "expert", 0, 0, tiled=True)
    gate_values_grad = jnp.sum(
        jnp.where(routes.T[None] == places[:, None, None], pair_back[:, None, :], 0.0), axis=0
    ).T

    units = shared_out.shape[0]
    column_normed, out_grad, in_grad, unit_in, unit_out = barrier(
        (column_normed, out_grad, in_grad, unit_in, unit_out)
    )
    unit_in = jnp.concatenate(gather_third(unit_in, group), axis=1)
    unit_out = jnp.concatenate(gather_third(unit_out, group), axis=0)
    expert_out_grad = lax.psum_scatter(out_grad, "dp", scatter_dimension=0, tiled=True)
    plane_units = group * units
    shared_weight = jax.nn.sigmoid(
        jnp.sum(column_normed.astype(F32) * gate_full, axis=1, keepdims=True)
    )
    unit_flat = unit_in.reshape(2 * plane_units, width)
    shared_pre = mm_nt(column_normed, unit_flat)
    s_gate, s_up = shared_pre[:, :plane_units], shared_pre[:, plane_units:]
    shared_act = swiglu_parts(s_gate, s_up)[1].astype(BF16)
    shared_val = mm(shared_act, unit_out)
    column_grad = column_cot.astype(F32) * column_valid
    shared_val_grad = (column_grad * shared_weight).astype(BF16)
    logit_grad = jnp.sum(column_grad * shared_val, axis=1, keepdims=True)
    logit_grad = logit_grad * shared_weight * (1.0 - shared_weight)
    gate_grad = jnp.sum(logit_grad * column_normed.astype(F32), axis=0)
    shared_act_grad = mm_nt(shared_val_grad, unit_out)
    shared_pre_grad = jnp.concatenate(swiglu_back(s_gate, s_up, shared_act_grad), axis=1)
    shared_pre_grad = shared_pre_grad.astype(BF16)
    normed_term = mm(shared_pre_grad, unit_flat) + logit_grad * gate_full
    normed_term, expert_out_grad = barrier((normed_term.astype(BF16), expert_out_grad))
    shared_grad = lax.psum_scatter(normed_term, "dp", scatter_dimension=0, tiled=True)
    shared_grad, in_grad = barrier((shared_grad, in_grad))
    shared_grad = shared_grad.astype(F32)
    expert_in_grad = lax.psum_scatter(in_grad, "dp", scatter_dimension=0, tiled=True)
    unit_out_grad = mm_tn(shared_act, shared_val_grad)
    unit_in_grad = mm_tn(shared_pre_grad, column_normed)
    shared_out_grad = plane_sum(unit_out_grad.reshape(group, units, width), group)
    unit_in_grad = unit_in_grad.reshape(2, group, units, width).transpose(1, 0, 2, 3)
    shared_in_grad = plane_sum(unit_in_grad, group).transpose(2, 0, 1)

    normed2_grad = shared_grad + routed_grad
    norm_term, norm2_part = norm_back(hidden, scale2, norm2_full, normed2_grad)
    hidden_grad = cotangent.astype(F32) * valid_float + norm_term
    branch_grad = plane_rows(hidden_grad.astype(BF16), group, order)

    out_own_grad = mm_tn(mixed, branch_grad).astype(BF16)
    out_own_grad = out_own_grad.reshape(own_heads, split, shard, width).transpose(1, 0, 2, 3)
    out_own_grad = lax.all_to_all(
        out_own_grad, "expert", 0, 0, axis_index_groups=pairs, tiled=True
    ).reshape(planes * shard, width)
    out_own = lax.dynamic_slice_in_dim(out_whole, me * own_width, own_width, 0)
    mixed_grad = mm_nt(branch_grad, out_own).astype(BF16).reshape(head_shape)
    value_grad = jnp.einsum(
        "shqk,sqhd->skhd", probs.astype(BF16), mixed_grad, preferred_element_type=F32
    )
    probs_grad = jnp.einsum("sqhd,skhd->shqk", mixed_grad, value, preferred_element_type=F32)
    score_grad = probs * (probs_grad - jnp.sum(probs_grad * probs, axis=-1, keepdims=True))
    score_grad = score_grad.astype(BF16)
    query_grad = jnp.einsum("shqk,skhd->sqhd", score_grad, key, preferred_element_type=F32)
    key_grad = jnp.einsum("shqk,sqhd->skhd", score_grad, query, preferred_element_type=F32)
    query_grad = rotate(query_grad * score_scale, cos_table, -sin_table)
    key_grad = rotate(key_grad * score_scale, cos_table, -sin_table)
    flat_shape = (group_rows, own_width)
    qkv_grad = jnp.concatenate(
        [
            query_grad.reshape(flat_shape),
            key_grad.reshape(flat_shape),
            value_grad.reshape(flat_shape),
        ],
        axis=1,
    ).astype(BF16)
    bias_part = jnp.sum(qkv_grad.astype(F32), axis=0)
    sent_grad = jnp.take(qkv_grad.reshape(group, rows, 3 * own_width), order_list, axis=0)
    normed1_grad = mm_nt(sent_grad.reshape(group_rows, 3 * own_width), qkv_own)
    normed1_grad = plane_sum(normed1_grad.reshape(group, rows, width), group)
    qkv_own_grad = mm_tn(normed1, qkv_grad).astype(BF16)
    shared_part = (shared_weight * shared_val).astype(BF16)
    shared_part, expert_in_grad = barrier((shared_part, expert_in_grad))
    shared_sum = lax.psum_scatter(shared_part, "dp", scatter_dimension=0, tiled=True)
    qkv_own_grad, shared_sum = barrier((qkv_own_grad, shared_sum))
    shared_sum = shared_sum.astype(F32)
    qkv_own_grad = lax.psum_scatter(qkv_own_grad, "dp", scatter_dimension=0, tiled=True)
    out_own_grad, qkv_own_grad = barrier((out_own_grad, qkv_own_grad))
    out_weight_grad = lax.psum_scatter(out_own_grad, "dp", scatter_dimension=0, tiled=True)
    output = (valid_float * (hidden + shared_sum + routed_sum)).astype(BF16)
    qkv_own_grad = lax.all_to_all(
        qkv_own_grad.reshape(group, shard, 3 * own_width), "expert", 0, 0, tiled=True
    )
    qkv_weight_grad = (
        qkv_own_grad.reshape(lanes, split, shard, 3, own_heads, HEAD)
        .transpose(2, 3, 1, 4, 0, 5)
        .reshape(shard, 3 * width)
        .astype(F32)
    )
    own_tokens = tokens.astype(F32)
    token_term, norm1_part = norm_back(own_tokens, norm_scale(own_tokens), norm1_full, normed1_grad)
    tokens_grad = hidden_grad + token_term

    here = (jnp.arange(split)[:, None] == part) & (jnp.arange(lanes)[None, :] == lane)
    bias_all = jnp.where(
        here[None, :, None, :, None], bias_part.reshape(3, 1, own_heads, 1, HEAD), 0.0
    ).reshape(devices, qkv_bias.shape[0])
    sums = jnp.concatenate(
        [
            norm1_part.reshape(devices, shard),
            norm2_part.reshape(devices, shard),
            gate_grad.reshape(devices, shard),
            bias_all,
        ],
        axis=1,
    )
    sums = jnp.pad(sums, ((0, 0), (0, vector_rows * 128 - sums.shape[1])))
    sums = lax.all_to_all(sums.reshape(devices, vector_rows, 128), both, 0, 0, tiled=True)
    sums = jnp.sum(sums, axis=0).reshape(-1)

    return (
        output,
        tokens_grad,
        sums[:shard],
        qkv_weight_grad,
        sums[3 * shard : 3 * shard + qkv_bias.shape[0]],
        out_weight_grad.astype(F32),
        sums[shard : 2 * shard],
        shared_in_grad,
        shared_out_grad,
        sums[2 * shard : 3 * shard],
        expert_in_grad.astype(F32)[None],
        expert_out_grad.astype(F32)[None],
        gate_values_grad,
    )


def solution(mesh):
    both = ("dp", "expert")
    in_specs = (
        P(both, None),
        P(both),
        P(both, None),
        P(both, None),
        P(both, None),
        P(both),
        P(both, None),
        P(both),
        P(both, None),
        P(both),
        P(None, None, both),
        P(both, None),
        P(both),
        P("expert", None, None),
        P("expert", None, None),
    )
    out_specs = (
        P(both, None),
        P(both, None),
        P(both),
        P(both, None),
        P(both),
        P(both, None),
        P(both),
        P(None, None, both),
        P(both, None),
        P(both),
        P("expert", "dp", None),
        P("expert", "dp", None),
        P(both, None),
    )
    return jax.shard_map(shards, mesh=mesh, in_specs=in_specs, out_specs=out_specs, check_vma=False)
```

```python
import functools
import math

import jax
import jax.numpy as jnp
import numpy as np
from jax import lax
from jax.experimental import pallas as pl
from jax.experimental.pallas import tpu as pltpu
from jax.sharding import PartitionSpec as P

HEAD = 128
NORM_EPS = 1e-06
THETA = 1000000.0
F32 = jnp.float32
barrier = lax.optimization_barrier
BF16 = jnp.bfloat16


def dot(a, b, dims):
    return lax.dot_general(a, b, (dims, ((), ())), preferred_element_type=F32)


def mm(a, b):
    return dot(a, b, ((1,), (0,)))


def mm_nt(a, b):
    return dot(a, b, ((1,), (1,)))


def mm_tn(a, b):
    return dot(a, b, ((0,), (0,)))


def plane_order(size, me):
    if size == 8:
        even, odd = [0, 2, 4, 6, 1, 5, 3, 7], [0, 4, 2, 6, 1, 3, 5, 7]
        first = me % 2 == 0
        return [me ^ (a if a == b else jnp.where(first, a, b)) for a, b in zip(even, odd)]
    return [me ^ m for m in range(size)]


def first_hop(i):
    return i ^ 2 if i % 2 == 0 else i ^ 4


def second_hop(i):
    return i ^ 4 if i % 2 == 0 else i ^ 2


def send(block, size, target):
    return lax.ppermute(block, "expert", [(i, target(i)) for i in range(size)])


def core_swap(i):
    return i ^ 1


def gather_first(block, size):
    if size == 8:
        return [block, send(block, size, first_hop), send(block, size, second_hop)]
    return [block] + [send(block, size, lambda i, m=m: i ^ m) for m in range(1, size)]


def gather_second(parts, size):
    return parts + [send(parts[1], size, second_hop)] if size == 8 else parts


def gather_third(parts, size):
    return parts + [send(part, size, core_swap) for part in parts] if size == 8 else parts


def plane_gather(block, size):
    return gather_third(gather_second(gather_first(block, size), size), size)


def plane_place(parts, order, whole, place):
    for j, part in enumerate(parts):
        whole = place(whole, part, order[j])
    return whole


def plane_rows(parts, order):
    rows = parts[0].shape[0]
    whole = jnp.zeros((len(parts) * rows,) + parts[0].shape[1:], parts[0].dtype)
    return plane_place(
        parts,
        order,
        whole,
        lambda whole, part, source: lax.dynamic_update_slice_in_dim(whole, part, source * rows, 0),
    )


def sum_first(near, far, size):
    if size == 8:
        return near.astype(F32) + send(far.astype(BF16), size, core_swap).astype(F32)
    parts = jnp.concatenate([near.astype(BF16), far.astype(BF16)], axis=0)
    parts = parts.reshape((size, parts.shape[0] // size) + parts.shape[1:])
    total = parts[0].astype(F32)
    for m in range(1, size):
        total = total + send(parts[m], size, lambda i, m=m: i ^ m).astype(F32)
    return total


def sum_hop(near, size, hop):
    if size != 8:
        return near
    half = near.shape[0] // 2
    return near[:half] + send(near[half:].astype(BF16), size, hop).astype(F32)


def plane_sum(near, far, size):
    near = sum_hop(sum_first(near, far, size), size, second_hop)
    return sum_hop(near, size, first_hop)


def norm_scale(rows):
    return lax.rsqrt(jnp.mean(rows * rows, axis=-1, keepdims=True) + NORM_EPS)


def norm_back(rows, scale, gain, grad):
    unit = rows * scale
    weighted = grad * gain
    inner = jnp.mean(weighted * unit, axis=-1, keepdims=True)
    return scale * (weighted - unit * inner), jnp.sum(grad * unit, axis=0)


def swiglu_parts(gate, up):
    sig = jax.nn.sigmoid(gate)
    return sig, gate * sig * up


def swiglu_back(gate, up, grad):
    sig = jax.nn.sigmoid(gate)
    silu = gate * sig
    return grad * up * (sig + silu * (1.0 - sig)), grad * silu


def rotary_tables(row_count):
    half = HEAD // 2
    powers = -(np.arange(half, dtype=np.float32) * np.float32(2.0)) / np.float32(HEAD)
    freqs = np.power(np.float32(THETA), powers).astype(np.float32)
    angles = np.arange(row_count, dtype=np.float32)[:, None] * freqs[None, :]
    cos, sin = np.cos(angles), np.sin(angles)
    return np.concatenate([cos, cos], axis=1), np.concatenate([-sin, sin], axis=1)


def head_probs(query, key, scale):
    scores = mm_nt(query, key) * scale
    shape = scores.shape
    causal = lax.broadcasted_iota(jnp.int32, shape, 0) >= lax.broadcasted_iota(jnp.int32, shape, 1)
    scores = jnp.where(causal, scores, -1e30)
    raised = jnp.exp(scores - jnp.max(scores, axis=-1, keepdims=True))
    return raised / jnp.sum(raised, axis=-1, keepdims=True)


def attend_kernel(
    heads, seq, tokens, gain, weight, bias, cos, sin, normed_out, qkv_out, mixed_out, lin
):
    rows = tokens[...].astype(F32)
    normed_out[...] = (rows * norm_scale(rows) * gain[...]).astype(BF16)
    lin[...] = mm(normed_out[...], weight[...]) + bias[...]
    for s in range(tokens.shape[0] // seq):
        row = slice(s * seq, (s + 1) * seq)
        for h in range(heads):
            low = []
            for kind in range(3):
                at = (kind * heads + h) * HEAD
                part = lin[row, at : at + HEAD]
                if kind < 2:
                    part = part * cos[...] + pltpu.roll(part, HEAD // 2, 1) * sin[...]
                low.append(part.astype(BF16))
                qkv_out[row, at : at + HEAD] = low[-1]
            probs = head_probs(low[0], low[1], 1.0 / math.sqrt(HEAD))
            mixed_out[row, h * HEAD : (h + 1) * HEAD] = mm(probs.astype(BF16), low[2]).astype(BF16)


def attend(tokens, gain, weight, bias, seq):
    total, width = tokens.shape
    wide = weight.shape[1]
    heads = wide // (3 * HEAD)
    rows = 4 * seq
    cos, sin = rotary_tables(seq)

    def whole(shape):
        return pl.BlockSpec(shape, lambda i: (0, 0))

    def block(columns):
        return pl.BlockSpec((rows, columns), lambda i: (i, 0))

    return pl.pallas_call(
        functools.partial(attend_kernel, heads, seq),
        grid=(total // rows,),
        in_specs=[
            block(width),
            whole((1, width)),
            whole((width, wide)),
            whole((1, wide)),
            whole((seq, HEAD)),
            whole((seq, HEAD)),
        ],
        out_specs=[block(width), block(wide), block(heads * HEAD)],
        out_shape=[
            jax.ShapeDtypeStruct((total, width), BF16),
            jax.ShapeDtypeStruct((total, wide), BF16),
            jax.ShapeDtypeStruct((total, heads * HEAD), BF16),
        ],
        scratch_shapes=[pltpu.VMEM((rows, wide), F32)],
        compiler_params=pltpu.CompilerParams(vmem_limit_bytes=48 << 20),
        name="attend",
    )(tokens, gain[None], weight, bias[None], jnp.asarray(cos), jnp.asarray(sin))


def attend_back_kernel(heads, size, order, *refs):
    parts, refs = refs[:size], refs[size:]
    qkv, mixed, out_own, weight, cos, sin = refs[:6]
    normed_grad, qkv_grad, out_grad, bias_grad, branch, mixed_grad, near_mixed, near_grad = refs[6:]
    seq = parts[0].shape[0]
    scale = 1.0 / math.sqrt(HEAD)
    for j, part in enumerate(parts):
        branch[j * seq : (j + 1) * seq, :] = part[...]
    mixed_grad[...] = mm_nt(branch[...], out_own[...]).astype(BF16)

    def one(j, carry):
        near = pl.ds(pl.multiple_of(j * seq, seq), seq)
        far = pl.ds(pl.multiple_of(order[j] * seq, seq), seq)
        near_mixed[near, :] = mixed[far, :]
        for h in range(heads):
            at = [(kind * heads + h) * HEAD for kind in range(3)]
            query, key, value = [qkv[far, a : a + HEAD] for a in at]
            grad = mixed_grad[near, h * HEAD : (h + 1) * HEAD]
            probs = head_probs(query, key, scale)
            value_grad = mm_tn(probs.astype(BF16), grad)
            probs_grad = mm_nt(grad, value)
            score_grad = probs * (probs_grad - jnp.sum(probs_grad * probs, axis=-1, keepdims=True))
            score_grad = score_grad.astype(BF16)
            turned = [mm(score_grad, key) * scale, mm_tn(score_grad, query) * scale]
            turned = [g * cos[...] - pltpu.roll(g, HEAD // 2, 1) * sin[...] for g in turned]
            for a, g in zip(at, turned + [value_grad]):
                low = g.astype(BF16)
                near_grad[near, a : a + HEAD] = low
                qkv_grad[far, a : a + HEAD] = low
        return carry

    lax.fori_loop(0, size, one, 0)
    normed_grad[...] = mm_nt(near_grad[...], weight[...]).astype(BF16)
    bias_grad[...] = jnp.sum(near_grad[...].astype(F32), axis=0, keepdims=True)
    out_grad[...] = mm_tn(near_mixed[...], branch[...]).astype(BF16)


def attend_back(order, parts, qkv, mixed, out_own, weight):
    size = len(parts)
    seq, width = parts[0].shape
    wide = weight.shape[1]
    own = wide // 3
    cos, sin = rotary_tables(seq)

    def whole(shape):
        return pl.BlockSpec(shape, lambda i, order: (0, 0))

    inputs = list(parts) + [qkv, mixed, out_own, weight, jnp.asarray(cos), jnp.asarray(sin)]
    shapes = [
        jax.ShapeDtypeStruct((size * seq, width), BF16),
        jax.ShapeDtypeStruct((size * seq, wide), BF16),
        jax.ShapeDtypeStruct((own, width), BF16),
        jax.ShapeDtypeStruct((1, wide), F32),
    ]
    return pl.pallas_call(
        functools.partial(attend_back_kernel, own // HEAD, size),
        grid_spec=pltpu.PrefetchScalarGridSpec(
            num_scalar_prefetch=1,
            grid=(1,),
            in_specs=[whole(a.shape) for a in inputs],
            out_specs=[whole(a.shape) for a in shapes],
            scratch_shapes=[
                pltpu.VMEM((size * seq, width), BF16),
                pltpu.VMEM((size * seq, own), BF16),
                pltpu.VMEM((size * seq, own), BF16),
                pltpu.VMEM((size * seq, wide), BF16),
            ],
        ),
        out_shape=shapes,
        compiler_params=pltpu.CompilerParams(vmem_limit_bytes=60 << 20),
        name="attend_back",
    )(order, *inputs)


def shards(
    tokens,
    lengths,
    routes,
    gate_values,
    cotangent,
    norm1_gain,
    qkv_weight,
    qkv_bias,
    out_weight,
    norm2_gain,
    shared_in,
    shared_out,
    shared_gate,
    expert_in,
    expert_out,
):
    rows, width = tokens.shape
    top = routes.shape[1]
    group = lax.axis_size("expert")
    planes = lax.axis_size("dp")
    devices = group * planes
    both = ("dp", "expert")
    me = lax.axis_index("expert")
    plane = lax.axis_index("dp")
    heads = width // HEAD
    own_heads = heads // group
    shard = qkv_weight.shape[0]
    split = HEAD // shard
    lanes = group // split
    experts = group * expert_in.shape[0]
    valid_total = 23 * rows * devices // 32
    capacity = 5 * valid_total * top // (4 * experts * planes)
    slots = -(-capacity // 16) * 16
    order = plane_order(group, me)
    order_list = jnp.stack(order)
    group_rows = group * rows

    vectors = jnp.concatenate([norm1_gain, norm2_gain, shared_gate, qkv_bias]).astype(F32)
    vector_rows = -(-vectors.shape[0] // 128)
    vectors = jnp.pad(vectors, (0, vector_rows * 128 - vectors.shape[0])).reshape(vector_rows, 128)
    info = jnp.concatenate(
        [
            vectors,
            routes.T.astype(F32),
            gate_values.T,
            jnp.broadcast_to(lengths.astype(F32)[:, None], (1, rows)),
        ],
        axis=0,
    )
    lane, part = me // split, me % split
    out_parts = lax.all_gather(out_weight[None], "dp", axis=0, tiled=True)
    by_head = qkv_weight.reshape(shard, 3, split, own_heads, lanes, HEAD)
    by_head = by_head.transpose(4, 2, 0, 1, 3, 5).reshape(group, shard, 3 * own_heads * HEAD)
    by_head = lax.all_to_all(by_head, "expert", 0, 0, tiled=True)
    by_head, token_source, cot_source = barrier((by_head, tokens, cotangent))
    out_parts, info = barrier((out_parts, info))
    qkv_own = lax.all_gather(by_head, "dp", axis=0, tiled=True).reshape(width, 3 * own_heads * HEAD)

    told = lax.all_to_all(
        jnp.broadcast_to(info[None], (devices,) + info.shape), both, 0, 0, tiled=True
    )
    flat = told[:, :vector_rows].reshape(devices, vector_rows * 128)
    norm1_full = flat[:, :shard].reshape(width)
    norm2_full = flat[:, shard : 2 * shard].reshape(width)
    gate_full = flat[:, 2 * shard : 3 * shard].reshape(width)
    bias_full = flat[:, 3 * shard : 3 * shard + qkv_bias.shape[0]].reshape(
        3, split, own_heads, lanes, HEAD
    )
    rest = told[:, vector_rows:].reshape(planes, group, 2 * top + 1, rows)
    column = lax.dynamic_index_in_dim(rest, me, 1, keepdims=False)
    slot = jnp.arange(rows, dtype=F32)
    all_routes = rest[:, :, :top].astype(jnp.int32)
    all_gates = rest[:, :, top : 2 * top]
    all_valid = slot < rest[:, :, 2 * top]
    column_valid = (slot[None, :] < column[:, 2 * top]).astype(F32).reshape(planes * rows, 1)
    valid_float = (slot < lengths.astype(F32)[0]).astype(F32)[:, None]

    bias_own = lax.dynamic_index_in_dim(bias_full, part, 1, keepdims=False)
    bias_own = lax.dynamic_index_in_dim(bias_own, lane, 2, keepdims=False).reshape(-1)
    pairs = [[k * split + p for p in range(split)] for k in range(lanes)]
    out_seen = gather_second(
        gather_first(out_parts.reshape(split, own_heads, shard, width), group), group
    )
    cot_seen = gather_second(gather_first(cot_source, group), group)
    group_tokens = plane_rows(plane_gather(token_source, group), order)
    group_tokens, unit_in = barrier((group_tokens, shared_in.transpose(1, 2, 0)))
    unit_in = gather_first(unit_in, group)
    qkv_own, column_source = barrier((qkv_own, cotangent))
    column_cot = lax.all_gather(column_source, "dp", axis=0, tiled=True)

    own_width = own_heads * HEAD
    positions = jnp.arange(rows, dtype=jnp.int32)
    places = jnp.arange(group, dtype=jnp.int32)
    normed1, qkv, mixed = attend(group_tokens, norm1_full, qkv_own, bias_own, rows)
    mixed, unit_in, out_seen = barrier((mixed, unit_in, out_seen))
    mixed_parts = gather_first(mixed, group)
    out_whole = plane_place(
        gather_third(out_seen, group),
        order,
        jnp.zeros((lanes, split, own_heads, split, shard, width), BF16),
        lambda whole, block, source: lax.dynamic_update_slice(
            whole, block[None, :, :, None], (source // split, 0, 0, source % split, 0, 0)
        ),
    ).reshape(width, width)

    mixed_parts, column_cot, cot_seen = barrier((mixed_parts, column_cot, cot_seen))
    mixed_parts = gather_third(gather_second(mixed_parts, group), group)
    group_cot = plane_rows(gather_third(cot_seen, group), order)
    mixed_whole = plane_place(
        mixed_parts,
        order,
        jnp.zeros((group_rows, width), BF16),
        lambda whole, block, source: lax.dynamic_update_slice(whole, block, (0, source * own_width)),
    )
    mixed_whole, unit_out = barrier((mixed_whole, shared_out))
    unit_out = gather_first(unit_out, group)
    group_hidden = group_tokens.astype(F32) + mm(mixed_whole, out_whole)
    group_scale2 = norm_scale(group_hidden)
    group_normed = (group_hidden * group_scale2 * norm2_full).astype(BF16)
    hidden = lax.dynamic_slice_in_dim(group_hidden, me * rows, rows, 0)
    scale2 = lax.dynamic_slice_in_dim(group_scale2, me * rows, rows, 0)
    normed2 = lax.dynamic_slice_in_dim(group_normed, me * rows, rows, 0)
    column_normed = lax.all_gather(normed2, "dp", axis=0, tiled=True)

    named = all_routes == me
    taken = jnp.any(named, axis=2) & all_valid
    gate_here = jnp.sum(jnp.where(named, all_gates, 0.0), axis=2)
    before = (positions[:, None] < positions[None, :]).astype(BF16)
    inside = mm(taken.astype(BF16).reshape(devices, rows), before).reshape(planes, group, rows)
    counts = jnp.sum(taken.astype(F32), axis=2)
    ahead = places[None, :] < places[:, None]
    offsets = jnp.sum(jnp.where(ahead[None], counts[:, None, :], 0.0), axis=2)
    all_rank = (inside + offsets[:, :, None]).astype(jnp.int32)
    all_rank = jnp.where(taken & (all_rank < capacity), all_rank, -1)
    rank = lax.dynamic_index_in_dim(all_rank, plane, 0, keepdims=False)
    gate_own = lax.dynamic_index_in_dim(gate_here, plane, 0, keepdims=False)
    slot_ids = jnp.arange(slots, dtype=jnp.int32)[:, None]
    chosen = rank.reshape(1, group_rows) == slot_ids
    pick = chosen.astype(BF16)
    put = (jnp.take(rank, order_list, axis=0).reshape(1, group_rows) == slot_ids).astype(BF16)
    put_near, put_far = put[:, : group_rows // 2], put[:, group_rows // 2 :]
    row_gate = jnp.sum(
        jnp.where(chosen, gate_own.reshape(1, group_rows), 0.0), axis=1, keepdims=True
    )
    weight_in, weight_out = expert_in[0], expert_out[0]
    hidden_units = weight_out.shape[0]
    expert_rows = mm(pick, group_normed).astype(BF16)
    expert_rows, unit_in, unit_out = barrier((expert_rows, unit_in, unit_out))
    unit_in, unit_out = gather_second(unit_in, group), gather_second(unit_out, group)
    cot_rows = mm(pick, group_cot)
    val_grad = (cot_rows * row_gate).astype(BF16)
    expert_pre = mm(expert_rows, weight_in)
    e_gate, e_up = expert_pre[:, :hidden_units], expert_pre[:, hidden_units:]
    expert_act = swiglu_parts(e_gate, e_up)[1].astype(BF16)
    act_grad = mm_nt(val_grad, weight_out)
    part_units = hidden_units // planes
    gated_act = (expert_act.astype(F32) * row_gate).astype(BF16)
    gated_act = gated_act.reshape(slots, planes, part_units).transpose(1, 0, 2)
    gated_act = lax.all_to_all(gated_act, "dp", 0, 0, tiled=True)
    pre_grad = jnp.concatenate(swiglu_back(e_gate, e_up, act_grad), axis=1).astype(BF16)
    in_gate = mm_tn(expert_rows, pre_grad[:, :hidden_units]).astype(BF16)
    in_gate, pre_grad, unit_in, unit_out = barrier((in_gate, pre_grad, unit_in, unit_out))
    unit_in = jnp.concatenate(gather_third(unit_in, group), axis=1)
    unit_out = jnp.concatenate(gather_third(unit_out, group), axis=0)
    in_up = mm_tn(expert_rows, pre_grad[:, hidden_units:]).astype(BF16)
    row_grad = mm_nt(pre_grad, weight_in).astype(BF16)
    expert_val = mm(expert_act, weight_out)
    pair_dot = jnp.sum(cot_rows * expert_val, axis=1, keepdims=True)
    gated_val = (expert_val * row_gate).astype(BF16)
    grad_far = mm_tn(put_far, row_grad).astype(BF16)
    grad_near = mm_tn(put_near, row_grad).astype(BF16)
    routed_grad = plane_sum(grad_near, grad_far, group)
    units = shared_out.shape[0]
    in_gate_grad = lax.psum_scatter(in_gate, "dp", scatter_dimension=0, tiled=True)
    column_normed, in_up = barrier((column_normed, in_up))
    cot_parts, unit_out = barrier((column_cot, unit_out))
    cot_parts = gather_first(cot_parts, group)
    plane_units = group * units
    shared_weight = jax.nn.sigmoid(
        jnp.sum(column_normed.astype(F32) * gate_full, axis=1, keepdims=True)
    )
    unit_flat = unit_in.reshape(2 * plane_units, width)
    shared_pre = mm_nt(column_normed, unit_flat)
    s_gate, s_up = shared_pre[:, :plane_units], shared_pre[:, plane_units:]
    shared_act = swiglu_parts(s_gate, s_up)[1].astype(BF16)
    shared_val = mm(shared_act, unit_out)
    column_grad = column_cot.astype(F32) * column_valid
    shared_val_grad = (column_grad * shared_weight).astype(BF16)
    logit_grad = jnp.sum(column_grad * shared_val, axis=1, keepdims=True)
    logit_grad = logit_grad * shared_weight * (1.0 - shared_weight)
    gate_grad = jnp.sum(logit_grad * column_normed.astype(F32), axis=0)
    shared_act_grad = mm_nt(shared_val_grad, unit_out)
    shared_pre_grad = jnp.concatenate(swiglu_back(s_gate, s_up, shared_act_grad), axis=1)
    shared_pre_grad = shared_pre_grad.astype(BF16)
    shared_pre_grad, cot_parts = barrier((shared_pre_grad, cot_parts))
    cot_parts = gather_second(cot_parts, group)
    normed_term = mm(shared_pre_grad, unit_flat) + logit_grad * gate_full
    normed_term, in_gate_grad, cot_parts, routed_grad, gated_act = barrier(
        (normed_term.astype(BF16), in_gate_grad, cot_parts, routed_grad, gated_act)
    )
    shared_grad = lax.psum_scatter(normed_term, "dp", scatter_dimension=0, tiled=True)
    cot_parts = gather_third(cot_parts, group)
    half_units = plane_units // 2
    unit_grads = []
    for left, right in (
        (shared_act, shared_val_grad),
        (shared_pre_grad[:, :plane_units], column_normed),
        (shared_pre_grad[:, plane_units:], column_normed),
    ):
        far = mm_tn(left[:, half_units:], right).astype(BF16)
        unit_grads.append((mm_tn(left[:, :half_units], right).astype(BF16), far))
    shared_grad, in_up, unit_grads, gated_val, pair_dot = barrier(
        (shared_grad, in_up, unit_grads, gated_val, pair_dot)
    )
    shared_grad = shared_grad.astype(F32)
    in_up_grad = lax.psum_scatter(in_up, "dp", scatter_dimension=0, tiled=True)
    normed2_grad = shared_grad + routed_grad
    norm_term, norm2_part = norm_back(hidden, scale2, norm2_full, normed2_grad)
    hidden_grad = cotangent.astype(F32) * valid_float + norm_term
    branch_parts = gather_first(hidden_grad.astype(BF16), group)
    unit_grads = [sum_first(near, far, group) for near, far in unit_grads]
    branch_parts, unit_grads = barrier((gather_second(branch_parts, group), unit_grads))
    branch_parts = gather_third(branch_parts, group)
    unit_grads = [sum_hop(total, group, second_hop) for total in unit_grads]

    out_own = lax.dynamic_slice_in_dim(out_whole, me * own_width, own_width, 0)
    normed1_grad, qkv_grad, out_own_grad, bias_part = attend_back(
        order_list, branch_parts, qkv, mixed, out_own, qkv_own
    )
    out_own_grad = out_own_grad.reshape(own_heads, split, shard, width).transpose(1, 0, 2, 3)
    out_own_grad = lax.all_to_all(
        out_own_grad, "expert", 0, 0, axis_index_groups=pairs, tiled=True
    ).reshape(planes, shard, width)
    qkv_grad, unit_grads[0] = barrier((qkv_grad, unit_grads[0]))
    qkv_own_grad = mm_tn(normed1, qkv_grad).astype(BF16)

    flat_rows = group * shard * 3 * own_width // width
    shared_part = (shared_weight * shared_val).astype(BF16).reshape(planes, rows, width)
    joined = jnp.concatenate(
        [qkv_own_grad.reshape(planes, flat_rows, width), out_own_grad, shared_part], axis=1
    )
    (
        normed1_grad,
        bias_part,
        unit_grads,
        gated_val,
        pair_dot,
        gated_act,
    ) = barrier(
        (
            normed1_grad,
            bias_part.reshape(-1),
            unit_grads,
            gated_val,
            pair_dot,
            gated_act,
        )
    )
    joined = lax.psum_scatter(joined, "dp", scatter_dimension=0, tiled=True)[0]
    half_rows = group_rows // 2
    normed1_grad = plane_sum(normed1_grad[:half_rows], normed1_grad[half_rows:], group)
    expert_in_grad = jnp.concatenate([in_gate_grad, in_up_grad], axis=1)
    out_weight_grad = joined[flat_rows : flat_rows + shard]
    shared_sum = joined[flat_rows + shard :].astype(F32)
    qkv_own_grad = joined[:flat_rows]
    qkv_own_grad = lax.all_to_all(
        qkv_own_grad.reshape(group, shard, 3 * own_width), "expert", 0, 0, tiled=True
    )
    qkv_weight_grad = (
        qkv_own_grad.reshape(lanes, split, shard, 3, own_heads, HEAD)
        .transpose(2, 3, 1, 4, 0, 5)
        .reshape(shard, 3 * width)
        .astype(F32)
    )
    own_tokens = tokens.astype(F32)
    token_term, norm1_part = norm_back(own_tokens, norm_scale(own_tokens), norm1_full, normed1_grad)
    tokens_grad = hidden_grad + token_term

    value_far = mm_tn(put_far, gated_val).astype(BF16)
    value_near = mm_tn(put_near, gated_val).astype(BF16)
    routed_sum = plane_sum(value_near, value_far, group)
    pair_dots = jnp.sum(jnp.where(chosen, pair_dot, 0.0), axis=0).reshape(group, rows)
    pair_back = lax.all_to_all(pair_dots, "expert", 0, 0, tiled=True)
    gate_values_grad = jnp.sum(
        jnp.where(routes.T[None] == places[:, None, None], pair_back[:, None, :], 0.0), axis=0
    ).T

    unit_grads, gated_act = barrier((unit_grads, gated_act))
    all_pick = (all_rank.reshape(planes, 1, group_rows) == slot_ids[None]).astype(BF16)
    token_act = lax.dot_general(
        all_pick, gated_act, (((1,), (1,)), ((0,), (0,))), preferred_element_type=F32
    )
    token_act = token_act.astype(BF16).reshape(planes, group, rows, part_units)
    expert_out_grad = 0.0
    for source, cot_part in zip(order, cot_parts):
        act_part = lax.dynamic_index_in_dim(token_act, source, 1, keepdims=False)
        expert_out_grad = expert_out_grad + mm_tn(
            act_part.reshape(planes * rows, part_units), cot_part
        )

    unit_grads = [sum_hop(total, group, first_hop) for total in unit_grads]
    shared_out_grad, gate_part, up_part = unit_grads
    shared_in_grad = jnp.stack([gate_part, up_part]).transpose(2, 0, 1)

    here = (jnp.arange(split)[:, None] == part) & (jnp.arange(lanes)[None, :] == lane)
    bias_all = jnp.where(
        here[None, :, None, :, None], bias_part.reshape(3, 1, own_heads, 1, HEAD), 0.0
    ).reshape(devices, qkv_bias.shape[0])
    sums = jnp.concatenate(
        [
            norm1_part.reshape(devices, shard),
            norm2_part.reshape(devices, shard),
            gate_grad.reshape(devices, shard),
            bias_all,
        ],
        axis=1,
    )
    sums = jnp.pad(sums, ((0, 0), (0, vector_rows * 128 - sums.shape[1])))
    sums = lax.all_to_all(sums.reshape(devices, vector_rows, 128), both, 0, 0, tiled=True)
    sums, shared_out_grad, shared_in_grad, routed_sum = barrier(
        (sums, shared_out_grad, shared_in_grad, routed_sum)
    )
    sums = jnp.sum(sums, axis=0).reshape(-1)

    output = (valid_float * (hidden + shared_sum + routed_sum)).astype(BF16)
    return (
        output,
        tokens_grad,
        sums[:shard],
        qkv_weight_grad,
        sums[3 * shard : 3 * shard + qkv_bias.shape[0]],
        out_weight_grad.astype(F32),
        sums[shard : 2 * shard],
        shared_in_grad,
        shared_out_grad,
        sums[2 * shard : 3 * shard],
        expert_in_grad.astype(F32)[None],
        expert_out_grad.astype(F32)[None],
        gate_values_grad,
    )


def solution(mesh):
    both = ("dp", "expert")
    in_specs = (
        P(both, None),
        P(both),
        P(both, None),
        P(both, None),
        P(both, None),
        P(both),
        P(both, None),
        P(both),
        P(both, None),
        P(both),
        P(None, None, both),
        P(both, None),
        P(both),
        P("expert", None, None),
        P("expert", None, None),
    )
    out_specs = (
        P(both, None),
        P(both, None),
        P(both),
        P(both, None),
        P(both),
        P(both, None),
        P(both),
        P(None, None, both),
        P(both, None),
        P(both),
        P("expert", "dp", None),
        P("expert", "dp", None),
        P(both, None),
    )
    return jax.shard_map(shards, mesh=mesh, in_specs=in_specs, out_specs=out_specs, check_vma=False)
```

```python
import functools
import math

import jax
import jax.numpy as jnp
import numpy as np
from jax import lax
from jax.experimental import pallas as pl
from jax.experimental.pallas import tpu as pltpu
from jax.sharding import PartitionSpec as P

HEAD = 128
NORM_EPS = 1e-06
THETA = 1000000.0
F32 = jnp.float32
barrier = lax.optimization_barrier
BF16 = jnp.bfloat16


def dot(a, b, dims):
    return lax.dot_general(a, b, (dims, ((), ())), preferred_element_type=F32)


def mm(a, b):
    return dot(a, b, ((1,), (0,)))


def mm_nt(a, b):
    return dot(a, b, ((1,), (1,)))


def mm_tn(a, b):
    return dot(a, b, ((0,), (0,)))


def plane_order(size, me):
    if size == 8:
        even, odd = [0, 2, 4, 6, 1, 5, 3, 7], [0, 4, 2, 6, 1, 3, 5, 7]
        first = me % 2 == 0
        return [me ^ (a if a == b else jnp.where(first, a, b)) for a, b in zip(even, odd)]
    return [me ^ m for m in range(size)]


def first_hop(i):
    return i ^ 2 if i % 2 == 0 else i ^ 4


def second_hop(i):
    return i ^ 4 if i % 2 == 0 else i ^ 2


def send(block, size, target):
    return lax.ppermute(block, "expert", [(i, target(i)) for i in range(size)])


def core_swap(i):
    return i ^ 1


def gather_first(block, size):
    if size == 8:
        return [block, send(block, size, first_hop), send(block, size, second_hop)]
    return [block] + [send(block, size, lambda i, m=m: i ^ m) for m in range(1, size)]


def gather_second(parts, size):
    return parts + [send(parts[1], size, second_hop)] if size == 8 else parts


def gather_third(parts, size):
    return parts + [send(part, size, core_swap) for part in parts] if size == 8 else parts


def plane_gather(block, size):
    return gather_third(gather_second(gather_first(block, size), size), size)


def plane_place(parts, order, whole, place):
    for j, part in enumerate(parts):
        whole = place(whole, part, order[j])
    return whole


def plane_rows(parts, order):
    rows = parts[0].shape[0]
    whole = jnp.zeros((len(parts) * rows,) + parts[0].shape[1:], parts[0].dtype)
    return plane_place(
        parts,
        order,
        whole,
        lambda whole, part, source: lax.dynamic_update_slice_in_dim(whole, part, source * rows, 0),
    )


def sum_first(near, far, size):
    if size == 8:
        return near.astype(F32) + send(far.astype(BF16), size, core_swap).astype(F32)
    parts = jnp.concatenate([near.astype(BF16), far.astype(BF16)], axis=0)
    parts = parts.reshape((size, parts.shape[0] // size) + parts.shape[1:])
    total = parts[0].astype(F32)
    for m in range(1, size):
        total = total + send(parts[m], size, lambda i, m=m: i ^ m).astype(F32)
    return total


def sum_hop(near, size, hop):
    if size != 8:
        return near
    half = near.shape[0] // 2
    return near[:half] + send(near[half:].astype(BF16), size, hop).astype(F32)


def plane_sum(near, far, size):
    near = sum_hop(sum_first(near, far, size), size, second_hop)
    return sum_hop(near, size, first_hop)


def norm_scale(rows):
    return lax.rsqrt(jnp.mean(rows * rows, axis=-1, keepdims=True) + NORM_EPS)


def norm_back(rows, scale, gain, grad):
    unit = rows * scale
    weighted = grad * gain
    inner = jnp.mean(weighted * unit, axis=-1, keepdims=True)
    return scale * (weighted - unit * inner), jnp.sum(grad * unit, axis=0)


def swiglu_parts(gate, up):
    sig = jax.nn.sigmoid(gate)
    return sig, gate * sig * up


def swiglu_back(gate, up, grad):
    sig = jax.nn.sigmoid(gate)
    silu = gate * sig
    return grad * up * (sig + silu * (1.0 - sig)), grad * silu


def rotary_tables(row_count):
    half = HEAD // 2
    powers = -(np.arange(half, dtype=np.float32) * np.float32(2.0)) / np.float32(HEAD)
    freqs = np.power(np.float32(THETA), powers).astype(np.float32)
    angles = np.arange(row_count, dtype=np.float32)[:, None] * freqs[None, :]
    cos, sin = np.cos(angles), np.sin(angles)
    return np.concatenate([cos, cos], axis=1), np.concatenate([-sin, sin], axis=1)


def head_probs(query, key, scale):
    scores = mm_nt(query, key) * scale
    shape = scores.shape
    causal = lax.broadcasted_iota(jnp.int32, shape, 0) >= lax.broadcasted_iota(jnp.int32, shape, 1)
    scores = jnp.where(causal, scores, -1e30)
    raised = jnp.exp(scores - jnp.max(scores, axis=-1, keepdims=True))
    return raised / jnp.sum(raised, axis=-1, keepdims=True)


def attend_kernel(
    heads, seq, tokens, gain, weight, bias, cos, sin, normed_out, qkv_out, mixed_out, lin
):
    rows = tokens[...].astype(F32)
    normed_out[...] = (rows * norm_scale(rows) * gain[...]).astype(BF16)
    lin[...] = mm(normed_out[...], weight[...]) + bias[...]
    for s in range(tokens.shape[0] // seq):
        row = slice(s * seq, (s + 1) * seq)
        for h in range(heads):
            low = []
            for kind in range(3):
                at = (kind * heads + h) * HEAD
                part = lin[row, at : at + HEAD]
                if kind < 2:
                    part = part * cos[...] + pltpu.roll(part, HEAD // 2, 1) * sin[...]
                low.append(part.astype(BF16))
                qkv_out[row, at : at + HEAD] = low[-1]
            probs = head_probs(low[0], low[1], 1.0 / math.sqrt(HEAD))
            mixed_out[row, h * HEAD : (h + 1) * HEAD] = mm(probs.astype(BF16), low[2]).astype(BF16)


def attend(tokens, gain, weight, bias, seq):
    total, width = tokens.shape
    wide = weight.shape[1]
    heads = wide // (3 * HEAD)
    rows = 4 * seq
    cos, sin = rotary_tables(seq)

    def whole(shape):
        return pl.BlockSpec(shape, lambda i: (0, 0))

    def block(columns):
        return pl.BlockSpec((rows, columns), lambda i: (i, 0))

    return pl.pallas_call(
        functools.partial(attend_kernel, heads, seq),
        grid=(total // rows,),
        in_specs=[
            block(width),
            whole((1, width)),
            whole((width, wide)),
            whole((1, wide)),
            whole((seq, HEAD)),
            whole((seq, HEAD)),
        ],
        out_specs=[block(width), block(wide), block(heads * HEAD)],
        out_shape=[
            jax.ShapeDtypeStruct((total, width), BF16),
            jax.ShapeDtypeStruct((total, wide), BF16),
            jax.ShapeDtypeStruct((total, heads * HEAD), BF16),
        ],
        scratch_shapes=[pltpu.VMEM((rows, wide), F32)],
        compiler_params=pltpu.CompilerParams(vmem_limit_bytes=48 << 20),
        name="attend",
    )(tokens, gain[None], weight, bias[None], jnp.asarray(cos), jnp.asarray(sin))


def attend_back_kernel(heads, size, order, *refs):
    parts, refs = refs[:size], refs[size:]
    qkv, mixed, out_own, weight, cos, sin = refs[:6]
    normed_grad, qkv_grad, out_grad, bias_grad, branch, mixed_grad, near_mixed, near_grad = refs[6:]
    seq = parts[0].shape[0]
    scale = 1.0 / math.sqrt(HEAD)
    for j, part in enumerate(parts):
        branch[j * seq : (j + 1) * seq, :] = part[...]
    mixed_grad[...] = mm_nt(branch[...], out_own[...]).astype(BF16)

    def one(j, carry):
        near = pl.ds(pl.multiple_of(j * seq, seq), seq)
        far = pl.ds(pl.multiple_of(order[j] * seq, seq), seq)
        near_mixed[near, :] = mixed[far, :]
        for h in range(heads):
            at = [(kind * heads + h) * HEAD for kind in range(3)]
            query, key, value = [qkv[far, a : a + HEAD] for a in at]
            grad = mixed_grad[near, h * HEAD : (h + 1) * HEAD]
            probs = head_probs(query, key, scale)
            value_grad = mm_tn(probs.astype(BF16), grad)
            probs_grad = mm_nt(grad, value)
            score_grad = probs * (probs_grad - jnp.sum(probs_grad * probs, axis=-1, keepdims=True))
            score_grad = score_grad.astype(BF16)
            turned = [mm(score_grad, key) * scale, mm_tn(score_grad, query) * scale]
            turned = [g * cos[...] - pltpu.roll(g, HEAD // 2, 1) * sin[...] for g in turned]
            for a, g in zip(at, turned + [value_grad]):
                low = g.astype(BF16)
                near_grad[near, a : a + HEAD] = low
                qkv_grad[far, a : a + HEAD] = low
        return carry

    lax.fori_loop(0, size, one, 0)
    normed_grad[...] = mm_nt(near_grad[...], weight[...]).astype(BF16)
    bias_grad[...] = jnp.sum(near_grad[...].astype(F32), axis=0, keepdims=True)
    out_grad[...] = mm_tn(near_mixed[...], branch[...]).astype(BF16)


def attend_back(order, parts, qkv, mixed, out_own, weight):
    size = len(parts)
    seq, width = parts[0].shape
    wide = weight.shape[1]
    own = wide // 3
    cos, sin = rotary_tables(seq)

    def whole(shape):
        return pl.BlockSpec(shape, lambda i, order: (0, 0))

    inputs = list(parts) + [qkv, mixed, out_own, weight, jnp.asarray(cos), jnp.asarray(sin)]
    shapes = [
        jax.ShapeDtypeStruct((size * seq, width), BF16),
        jax.ShapeDtypeStruct((size * seq, wide), BF16),
        jax.ShapeDtypeStruct((own, width), BF16),
        jax.ShapeDtypeStruct((1, wide), F32),
    ]
    return pl.pallas_call(
        functools.partial(attend_back_kernel, own // HEAD, size),
        grid_spec=pltpu.PrefetchScalarGridSpec(
            num_scalar_prefetch=1,
            grid=(1,),
            in_specs=[whole(a.shape) for a in inputs],
            out_specs=[whole(a.shape) for a in shapes],
            scratch_shapes=[
                pltpu.VMEM((size * seq, width), BF16),
                pltpu.VMEM((size * seq, own), BF16),
                pltpu.VMEM((size * seq, own), BF16),
                pltpu.VMEM((size * seq, wide), BF16),
            ],
        ),
        out_shape=shapes,
        compiler_params=pltpu.CompilerParams(vmem_limit_bytes=60 << 20),
        name="attend_back",
    )(order, *inputs)


def shards(
    tokens,
    lengths,
    routes,
    gate_values,
    cotangent,
    norm1_gain,
    qkv_weight,
    qkv_bias,
    out_weight,
    norm2_gain,
    shared_in,
    shared_out,
    shared_gate,
    expert_in,
    expert_out,
):
    rows, width = tokens.shape
    top = routes.shape[1]
    group = lax.axis_size("expert")
    planes = lax.axis_size("dp")
    devices = group * planes
    both = ("dp", "expert")
    me = lax.axis_index("expert")
    plane = lax.axis_index("dp")
    heads = width // HEAD
    own_heads = heads // group
    shard = qkv_weight.shape[0]
    split = HEAD // shard
    lanes = group // split
    experts = group * expert_in.shape[0]
    valid_total = 23 * rows * devices // 32
    capacity = 5 * valid_total * top // (4 * experts * planes)
    slots = -(-capacity // 16) * 16
    order = plane_order(group, me)
    order_list = jnp.stack(order)
    group_rows = group * rows

    vectors = jnp.concatenate([norm1_gain, norm2_gain, shared_gate, qkv_bias]).astype(F32)
    vector_rows = -(-vectors.shape[0] // 128)
    vectors = jnp.pad(vectors, (0, vector_rows * 128 - vectors.shape[0])).reshape(vector_rows, 128)
    info = jnp.concatenate(
        [
            vectors,
            routes.T.astype(F32),
            gate_values.T,
            jnp.broadcast_to(lengths.astype(F32)[:, None], (1, rows)),
        ],
        axis=0,
    )
    lane, part = me // split, me % split
    out_parts = lax.all_gather(out_weight[None], "dp", axis=0, tiled=True)
    by_head = qkv_weight.reshape(shard, 3, split, own_heads, lanes, HEAD)
    by_head = by_head.transpose(4, 2, 0, 1, 3, 5).reshape(group, shard, 3 * own_heads * HEAD)
    by_head = lax.all_to_all(by_head, "expert", 0, 0, tiled=True)
    by_head, token_source, cot_source = barrier((by_head, tokens, cotangent))
    out_parts, info = barrier((out_parts, info))
    qkv_own = lax.all_gather(by_head, "dp", axis=0, tiled=True).reshape(width, 3 * own_heads * HEAD)

    told = lax.all_to_all(
        jnp.broadcast_to(info[None], (devices,) + info.shape), both, 0, 0, tiled=True
    )
    flat = told[:, :vector_rows].reshape(devices, vector_rows * 128)
    norm1_full = flat[:, :shard].reshape(width)
    norm2_full = flat[:, shard : 2 * shard].reshape(width)
    gate_full = flat[:, 2 * shard : 3 * shard].reshape(width)
    bias_full = flat[:, 3 * shard : 3 * shard + qkv_bias.shape[0]].reshape(
        3, split, own_heads, lanes, HEAD
    )
    rest = told[:, vector_rows:].reshape(planes, group, 2 * top + 1, rows)
    column = lax.dynamic_index_in_dim(rest, me, 1, keepdims=False)
    slot = jnp.arange(rows, dtype=F32)
    all_routes = rest[:, :, :top].astype(jnp.int32)
    all_gates = rest[:, :, top : 2 * top]
    all_valid = slot < rest[:, :, 2 * top]
    column_valid = (slot[None, :] < column[:, 2 * top]).astype(F32).reshape(planes * rows, 1)
    valid_float = (slot < lengths.astype(F32)[0]).astype(F32)[:, None]

    bias_own = lax.dynamic_index_in_dim(bias_full, part, 1, keepdims=False)
    bias_own = lax.dynamic_index_in_dim(bias_own, lane, 2, keepdims=False).reshape(-1)
    pairs = [[k * split + p for p in range(split)] for k in range(lanes)]
    out_seen = gather_second(
        gather_first(out_parts.reshape(split, own_heads, shard, width), group), group
    )
    cot_seen = gather_second(gather_first(cot_source, group), group)
    group_tokens = plane_rows(plane_gather(token_source, group), order)
    group_tokens, unit_in = barrier((group_tokens, shared_in.transpose(1, 2, 0)))
    unit_in = gather_first(unit_in, group)
    qkv_own, column_source = barrier((qkv_own, cotangent))
    column_cot = lax.all_gather(column_source, "dp", axis=0, tiled=True)

    own_width = own_heads * HEAD
    positions = jnp.arange(rows, dtype=jnp.int32)
    places = jnp.arange(group, dtype=jnp.int32)
    normed1, qkv, mixed = attend(group_tokens, norm1_full, qkv_own, bias_own, rows)
    mixed, unit_in, out_seen = barrier((mixed, unit_in, out_seen))
    mixed_parts = gather_first(mixed, group)
    out_whole = plane_place(
        gather_third(out_seen, group),
        order,
        jnp.zeros((lanes, split, own_heads, split, shard, width), BF16),
        lambda whole, block, source: lax.dynamic_update_slice(
            whole, block[None, :, :, None], (source // split, 0, 0, source % split, 0, 0)
        ),
    ).reshape(width, width)

    mixed_parts, column_cot, cot_seen = barrier((mixed_parts, column_cot, cot_seen))
    mixed_parts = gather_third(gather_second(mixed_parts, group), group)
    group_cot = plane_rows(gather_third(cot_seen, group), order)
    mixed_whole = plane_place(
        mixed_parts,
        order,
        jnp.zeros((group_rows, width), BF16),
        lambda whole, block, source: lax.dynamic_update_slice(whole, block, (0, source * own_width)),
    )
    mixed_whole, unit_out = barrier((mixed_whole, shared_out))
    unit_out = gather_first(unit_out, group)
    group_hidden = group_tokens.astype(F32) + mm(mixed_whole, out_whole)
    group_scale2 = norm_scale(group_hidden)
    group_normed = (group_hidden * group_scale2 * norm2_full).astype(BF16)
    hidden = lax.dynamic_slice_in_dim(group_hidden, me * rows, rows, 0)
    scale2 = lax.dynamic_slice_in_dim(group_scale2, me * rows, rows, 0)
    normed2 = lax.dynamic_slice_in_dim(group_normed, me * rows, rows, 0)
    column_normed = lax.all_gather(normed2, "dp", axis=0, tiled=True)

    named = all_routes == me
    taken = jnp.any(named, axis=2) & all_valid
    gate_here = jnp.sum(jnp.where(named, all_gates, 0.0), axis=2)
    before = (positions[:, None] < positions[None, :]).astype(BF16)
    inside = mm(taken.astype(BF16).reshape(devices, rows), before).reshape(planes, group, rows)
    counts = jnp.sum(taken.astype(F32), axis=2)
    ahead = places[None, :] < places[:, None]
    offsets = jnp.sum(jnp.where(ahead[None], counts[:, None, :], 0.0), axis=2)
    all_rank = (inside + offsets[:, :, None]).astype(jnp.int32)
    all_rank = jnp.where(taken & (all_rank < capacity), all_rank, -1)
    rank = lax.dynamic_index_in_dim(all_rank, plane, 0, keepdims=False)
    gate_own = lax.dynamic_index_in_dim(gate_here, plane, 0, keepdims=False)
    slot_ids = jnp.arange(slots, dtype=jnp.int32)[:, None]
    chosen = rank.reshape(1, group_rows) == slot_ids
    pick = chosen.astype(BF16)
    put = (jnp.take(rank, order_list, axis=0).reshape(1, group_rows) == slot_ids).astype(BF16)
    put_near, put_far = put[:, : group_rows // 2], put[:, group_rows // 2 :]
    row_gate = jnp.sum(
        jnp.where(chosen, gate_own.reshape(1, group_rows), 0.0), axis=1, keepdims=True
    )
    weight_in, weight_out = expert_in[0], expert_out[0]
    hidden_units = weight_out.shape[0]
    expert_rows = mm(pick, group_normed).astype(BF16)
    expert_rows, unit_in, unit_out = barrier((expert_rows, unit_in, unit_out))
    unit_in, unit_out = gather_second(unit_in, group), gather_second(unit_out, group)
    cot_rows = mm(pick, group_cot)
    val_grad = (cot_rows * row_gate).astype(BF16)
    expert_pre = mm(expert_rows, weight_in)
    e_gate, e_up = expert_pre[:, :hidden_units], expert_pre[:, hidden_units:]
    expert_act = swiglu_parts(e_gate, e_up)[1].astype(BF16)
    act_grad = mm_nt(val_grad, weight_out)
    part_units = hidden_units // planes
    gated_act = (expert_act.astype(F32) * row_gate).astype(BF16)
    gated_act = gated_act.reshape(slots, planes, part_units).transpose(1, 0, 2)
    gated_act = lax.all_to_all(gated_act, "dp", 0, 0, tiled=True)
    pre_grad = jnp.concatenate(swiglu_back(e_gate, e_up, act_grad), axis=1).astype(BF16)
    in_gate = mm_tn(expert_rows, pre_grad[:, :hidden_units]).astype(BF16)
    in_gate, pre_grad, unit_in, unit_out = barrier((in_gate, pre_grad, unit_in, unit_out))
    unit_in = jnp.concatenate(gather_third(unit_in, group), axis=1)
    unit_out = jnp.concatenate(gather_third(unit_out, group), axis=0)
    in_up = mm_tn(expert_rows, pre_grad[:, hidden_units:]).astype(BF16)
    row_grad = mm_nt(pre_grad, weight_in).astype(BF16)
    expert_val = mm(expert_act, weight_out)
    pair_dot = jnp.sum(cot_rows * expert_val, axis=1, keepdims=True)
    gated_val = (expert_val * row_gate).astype(BF16)
    grad_far = mm_tn(put_far, row_grad).astype(BF16)
    grad_near = mm_tn(put_near, row_grad).astype(BF16)
    routed_grad = plane_sum(grad_near, grad_far, group)
    units = shared_out.shape[0]
    in_gate_grad = lax.psum_scatter(in_gate, "dp", scatter_dimension=0, tiled=True)
    column_normed, in_up = barrier((column_normed, in_up))
    cot_parts, unit_out = barrier((column_cot, unit_out))
    cot_parts = gather_first(cot_parts, group)
    plane_units = group * units
    shared_weight = jax.nn.sigmoid(
        jnp.sum(column_normed.astype(F32) * gate_full, axis=1, keepdims=True)
    )
    unit_flat = unit_in.reshape(2 * plane_units, width)
    shared_pre = mm_nt(column_normed, unit_flat)
    s_gate, s_up = shared_pre[:, :plane_units], shared_pre[:, plane_units:]
    shared_act = swiglu_parts(s_gate, s_up)[1].astype(BF16)
    shared_val = mm(shared_act, unit_out)
    column_grad = column_cot.astype(F32) * column_valid
    shared_val_grad = (column_grad * shared_weight).astype(BF16)
    logit_grad = jnp.sum(column_grad * shared_val, axis=1, keepdims=True)
    logit_grad = logit_grad * shared_weight * (1.0 - shared_weight)
    gate_grad = jnp.sum(logit_grad * column_normed.astype(F32), axis=0)
    shared_act_grad = mm_nt(shared_val_grad, unit_out)
    shared_pre_grad = jnp.concatenate(swiglu_back(s_gate, s_up, shared_act_grad), axis=1)
    shared_pre_grad = shared_pre_grad.astype(BF16)
    shared_pre_grad, cot_parts = barrier((shared_pre_grad, cot_parts))
    cot_parts = gather_second(cot_parts, group)
    normed_term = mm(shared_pre_grad, unit_flat) + logit_grad * gate_full
    normed_term, in_gate_grad, routed_grad, gated_act = barrier(
        (normed_term.astype(BF16), in_gate_grad, routed_grad, gated_act)
    )
    shared_grad = lax.psum_scatter(normed_term, "dp", scatter_dimension=0, tiled=True)
    half_units = plane_units // 2
    unit_grads = []
    for left, right in (
        (shared_act, shared_val_grad),
        (shared_pre_grad[:, :plane_units], column_normed),
        (shared_pre_grad[:, plane_units:], column_normed),
    ):
        far = mm_tn(left[:, half_units:], right).astype(BF16)
        unit_grads.append((mm_tn(left[:, :half_units], right).astype(BF16), far))
    shared_grad, in_up, unit_grads, gated_val, pair_dot, cot_parts = barrier(
        (shared_grad, in_up, unit_grads, gated_val, pair_dot, cot_parts)
    )
    cot_parts = gather_third(cot_parts, group)
    shared_grad = shared_grad.astype(F32)
    in_up_grad = lax.psum_scatter(in_up, "dp", scatter_dimension=0, tiled=True)
    normed2_grad = shared_grad + routed_grad
    norm_term, norm2_part = norm_back(hidden, scale2, norm2_full, normed2_grad)
    hidden_grad = cotangent.astype(F32) * valid_float + norm_term
    branch_parts = gather_first(hidden_grad.astype(BF16), group)
    unit_grads = [sum_first(near, far, group) for near, far in unit_grads]
    branch_parts, unit_grads = barrier((gather_second(branch_parts, group), unit_grads))
    branch_parts = gather_third(branch_parts, group)
    unit_grads = [sum_hop(total, group, second_hop) for total in unit_grads]

    out_own = lax.dynamic_slice_in_dim(out_whole, me * own_width, own_width, 0)
    normed1_grad, qkv_grad, out_own_grad, bias_part = attend_back(
        order_list, branch_parts, qkv, mixed, out_own, qkv_own
    )
    out_own_grad = out_own_grad.reshape(own_heads, split, shard, width).transpose(1, 0, 2, 3)
    out_own_grad = lax.all_to_all(
        out_own_grad, "expert", 0, 0, axis_index_groups=pairs, tiled=True
    ).reshape(planes, shard, width)
    qkv_grad, unit_grads[0] = barrier((qkv_grad, unit_grads[0]))
    qkv_own_grad = mm_tn(normed1, qkv_grad).astype(BF16)

    flat_rows = group * shard * 3 * own_width // width
    shared_part = (shared_weight * shared_val).astype(BF16).reshape(planes, rows, width)
    joined = jnp.concatenate(
        [qkv_own_grad.reshape(planes, flat_rows, width), out_own_grad, shared_part], axis=1
    )
    (
        normed1_grad,
        bias_part,
        unit_grads,
        gated_val,
        pair_dot,
        gated_act,
    ) = barrier(
        (
            normed1_grad,
            bias_part.reshape(-1),
            unit_grads,
            gated_val,
            pair_dot,
            gated_act,
        )
    )
    joined = lax.psum_scatter(joined, "dp", scatter_dimension=0, tiled=True)[0]
    half_rows = group_rows // 2
    normed1_grad = plane_sum(normed1_grad[:half_rows], normed1_grad[half_rows:], group)
    expert_in_grad = jnp.concatenate([in_gate_grad, in_up_grad], axis=1).astype(F32)
    out_weight_grad = joined[flat_rows : flat_rows + shard]
    shared_sum = joined[flat_rows + shard :].astype(F32)
    qkv_own_grad = joined[:flat_rows]
    qkv_own_grad = lax.all_to_all(
        qkv_own_grad.reshape(group, shard, 3 * own_width), "expert", 0, 0, tiled=True
    )
    qkv_weight_grad = (
        qkv_own_grad.reshape(lanes, split, shard, 3, own_heads, HEAD)
        .transpose(2, 3, 1, 4, 0, 5)
        .reshape(shard, 3 * width)
        .astype(F32)
    )
    own_tokens = tokens.astype(F32)
    token_term, norm1_part = norm_back(own_tokens, norm_scale(own_tokens), norm1_full, normed1_grad)
    tokens_grad = hidden_grad + token_term

    value_far = mm_tn(put_far, gated_val).astype(BF16)
    value_near = mm_tn(put_near, gated_val).astype(BF16)
    routed_sum = plane_sum(value_near, value_far, group)
    pair_dots = jnp.sum(jnp.where(chosen, pair_dot, 0.0), axis=0).reshape(group, rows)
    pair_back = lax.all_to_all(pair_dots, "expert", 0, 0, tiled=True)
    gate_values_grad = jnp.sum(
        jnp.where(routes.T[None] == places[:, None, None], pair_back[:, None, :], 0.0), axis=0
    ).T

    unit_grads, gated_act, expert_in_grad = barrier((unit_grads, gated_act, expert_in_grad))
    all_pick = (all_rank.reshape(planes, 1, group_rows) == slot_ids[None]).astype(BF16)
    token_act = lax.dot_general(
        all_pick, gated_act, (((1,), (1,)), ((0,), (0,))), preferred_element_type=F32
    )
    token_act = token_act.astype(BF16).reshape(planes, group, rows, part_units)
    expert_out_grad = 0.0
    for source, cot_part in zip(order, cot_parts):
        act_part = lax.dynamic_index_in_dim(token_act, source, 1, keepdims=False)
        expert_out_grad = expert_out_grad + mm_tn(
            act_part.reshape(planes * rows, part_units), cot_part
        )

    unit_grads = [sum_hop(total, group, first_hop) for total in unit_grads]
    shared_out_grad, gate_part, up_part = unit_grads
    shared_in_grad = jnp.stack([gate_part, up_part]).transpose(2, 0, 1)

    here = (jnp.arange(split)[:, None] == part) & (jnp.arange(lanes)[None, :] == lane)
    bias_all = jnp.where(
        here[None, :, None, :, None], bias_part.reshape(3, 1, own_heads, 1, HEAD), 0.0
    ).reshape(devices, qkv_bias.shape[0])
    sums = jnp.concatenate(
        [
            norm1_part.reshape(devices, shard),
            norm2_part.reshape(devices, shard),
            gate_grad.reshape(devices, shard),
            bias_all,
        ],
        axis=1,
    )
    sums = jnp.pad(sums, ((0, 0), (0, vector_rows * 128 - sums.shape[1])))
    sums = lax.all_to_all(sums.reshape(devices, vector_rows, 128), both, 0, 0, tiled=True)
    sums, shared_out_grad, shared_in_grad, routed_sum = barrier(
        (sums, shared_out_grad, shared_in_grad, routed_sum)
    )
    sums = jnp.sum(sums, axis=0).reshape(-1)

    output = (valid_float * (hidden + shared_sum + routed_sum)).astype(BF16)
    return (
        output,
        tokens_grad,
        sums[:shard],
        qkv_weight_grad,
        sums[3 * shard : 3 * shard + qkv_bias.shape[0]],
        out_weight_grad.astype(F32),
        sums[shard : 2 * shard],
        shared_in_grad,
        shared_out_grad,
        sums[2 * shard : 3 * shard],
        expert_in_grad[None],
        expert_out_grad.astype(F32)[None],
        gate_values_grad,
    )


def solution(mesh):
    both = ("dp", "expert")
    in_specs = (
        P(both, None),
        P(both),
        P(both, None),
        P(both, None),
        P(both, None),
        P(both),
        P(both, None),
        P(both),
        P(both, None),
        P(both),
        P(None, None, both),
        P(both, None),
        P(both),
        P("expert", None, None),
        P("expert", None, None),
    )
    out_specs = (
        P(both, None),
        P(both, None),
        P(both),
        P(both, None),
        P(both),
        P(both, None),
        P(both),
        P(None, None, both),
        P(both, None),
        P(both),
        P("expert", "dp", None),
        P("expert", "dp", None),
        P(both, None),
    )
    return jax.shard_map(shards, mesh=mesh, in_specs=in_specs, out_specs=out_specs, check_vma=False)
```

```python
import functools
import math

import jax
import jax.numpy as jnp
import numpy as np
from jax import lax
from jax.experimental import pallas as pl
from jax.experimental.pallas import tpu as pltpu
from jax.sharding import PartitionSpec as P

HEAD = 128
NORM_EPS = 1e-06
THETA = 1000000.0
F32 = jnp.float32
barrier = lax.optimization_barrier
BF16 = jnp.bfloat16


def dot(a, b, dims):
    return lax.dot_general(a, b, (dims, ((), ())), preferred_element_type=F32)


def mm(a, b):
    return dot(a, b, ((1,), (0,)))


def mm_nt(a, b):
    return dot(a, b, ((1,), (1,)))


def mm_tn(a, b):
    return dot(a, b, ((0,), (0,)))


def plane_order(size, me):
    if size == 8:
        even, odd = [0, 2, 4, 6, 1, 5, 3, 7], [0, 4, 2, 6, 1, 3, 5, 7]
        first = me % 2 == 0
        return [me ^ (a if a == b else jnp.where(first, a, b)) for a, b in zip(even, odd)]
    return [me ^ m for m in range(size)]


def first_hop(i):
    return i ^ 2 if i % 2 == 0 else i ^ 4


def second_hop(i):
    return i ^ 4 if i % 2 == 0 else i ^ 2


def send(block, size, target):
    return lax.ppermute(block, "expert", [(i, target(i)) for i in range(size)])


def core_swap(i):
    return i ^ 1


def gather_first(block, size):
    if size == 8:
        return [block, send(block, size, first_hop), send(block, size, second_hop)]
    return [block] + [send(block, size, lambda i, m=m: i ^ m) for m in range(1, size)]


def gather_second(parts, size):
    return parts + [send(parts[1], size, second_hop)] if size == 8 else parts


def gather_third(parts, size):
    return parts + [send(part, size, core_swap) for part in parts] if size == 8 else parts


def plane_gather(block, size):
    return gather_third(gather_second(gather_first(block, size), size), size)


def plane_place(parts, order, whole, place):
    for j, part in enumerate(parts):
        whole = place(whole, part, order[j])
    return whole


def plane_rows(parts, order):
    rows = parts[0].shape[0]
    whole = jnp.zeros((len(parts) * rows,) + parts[0].shape[1:], parts[0].dtype)
    return plane_place(
        parts,
        order,
        whole,
        lambda whole, part, source: lax.dynamic_update_slice_in_dim(whole, part, source * rows, 0),
    )


def sum_first(near, far, size):
    if size == 8:
        return near.astype(F32) + send(far.astype(BF16), size, core_swap).astype(F32)
    parts = jnp.concatenate([near.astype(BF16), far.astype(BF16)], axis=0)
    parts = parts.reshape((size, parts.shape[0] // size) + parts.shape[1:])
    total = parts[0].astype(F32)
    for m in range(1, size):
        total = total + send(parts[m], size, lambda i, m=m: i ^ m).astype(F32)
    return total


def sum_hop(near, size, hop):
    if size != 8:
        return near
    half = near.shape[0] // 2
    return near[:half] + send(near[half:].astype(BF16), size, hop).astype(F32)


def plane_sum(near, far, size):
    near = sum_hop(sum_first(near, far, size), size, second_hop)
    return sum_hop(near, size, first_hop)


def norm_scale(rows):
    return lax.rsqrt(jnp.mean(rows * rows, axis=-1, keepdims=True) + NORM_EPS)


def norm_back(rows, scale, gain, grad):
    unit = rows * scale
    weighted = grad * gain
    inner = jnp.mean(weighted * unit, axis=-1, keepdims=True)
    return scale * (weighted - unit * inner), jnp.sum(grad * unit, axis=0)


def swiglu_parts(gate, up):
    sig = jax.nn.sigmoid(gate)
    return sig, gate * sig * up


def swiglu_back(gate, up, grad):
    sig = jax.nn.sigmoid(gate)
    silu = gate * sig
    return grad * up * (sig + silu * (1.0 - sig)), grad * silu


def rotary_tables(row_count):
    half = HEAD // 2
    powers = -(np.arange(half, dtype=np.float32) * np.float32(2.0)) / np.float32(HEAD)
    freqs = np.power(np.float32(THETA), powers).astype(np.float32)
    angles = np.arange(row_count, dtype=np.float32)[:, None] * freqs[None, :]
    cos, sin = np.cos(angles), np.sin(angles)
    return np.concatenate([cos, cos], axis=1), np.concatenate([-sin, sin], axis=1)


def head_probs(query, key, scale):
    scores = mm_nt(query, key) * scale
    shape = scores.shape
    causal = lax.broadcasted_iota(jnp.int32, shape, 0) >= lax.broadcasted_iota(jnp.int32, shape, 1)
    scores = jnp.where(causal, scores, -1e30)
    raised = jnp.exp(scores - jnp.max(scores, axis=-1, keepdims=True))
    return raised / jnp.sum(raised, axis=-1, keepdims=True)


def attend_kernel(
    heads, seq, tokens, gain, weight, bias, cos, sin, normed_out, qkv_out, mixed_out, lin
):
    rows = tokens[...].astype(F32)
    normed_out[...] = (rows * norm_scale(rows) * gain[...]).astype(BF16)
    lin[...] = mm(normed_out[...], weight[...]) + bias[...]
    for s in range(tokens.shape[0] // seq):
        row = slice(s * seq, (s + 1) * seq)
        for h in range(heads):
            low = []
            for kind in range(3):
                at = (kind * heads + h) * HEAD
                part = lin[row, at : at + HEAD]
                if kind < 2:
                    part = part * cos[...] + pltpu.roll(part, HEAD // 2, 1) * sin[...]
                low.append(part.astype(BF16))
                qkv_out[row, at : at + HEAD] = low[-1]
            probs = head_probs(low[0], low[1], 1.0 / math.sqrt(HEAD))
            mixed_out[row, h * HEAD : (h + 1) * HEAD] = mm(probs.astype(BF16), low[2]).astype(BF16)


def attend(tokens, gain, weight, bias, seq):
    total, width = tokens.shape
    wide = weight.shape[1]
    heads = wide // (3 * HEAD)
    rows = 4 * seq
    cos, sin = rotary_tables(seq)

    def whole(shape):
        return pl.BlockSpec(shape, lambda i: (0, 0))

    def block(columns):
        return pl.BlockSpec((rows, columns), lambda i: (i, 0))

    return pl.pallas_call(
        functools.partial(attend_kernel, heads, seq),
        grid=(total // rows,),
        in_specs=[
            block(width),
            whole((1, width)),
            whole((width, wide)),
            whole((1, wide)),
            whole((seq, HEAD)),
            whole((seq, HEAD)),
        ],
        out_specs=[block(width), block(wide), block(heads * HEAD)],
        out_shape=[
            jax.ShapeDtypeStruct((total, width), BF16),
            jax.ShapeDtypeStruct((total, wide), BF16),
            jax.ShapeDtypeStruct((total, heads * HEAD), BF16),
        ],
        scratch_shapes=[pltpu.VMEM((rows, wide), F32)],
        compiler_params=pltpu.CompilerParams(vmem_limit_bytes=48 << 20),
        name="attend",
    )(tokens, gain[None], weight, bias[None], jnp.asarray(cos), jnp.asarray(sin))


def attend_back_kernel(heads, size, order, *refs):
    parts, refs = refs[:size], refs[size:]
    qkv, mixed, out_own, weight, cos, sin = refs[:6]
    normed_grad, qkv_grad, out_grad, bias_grad, branch, mixed_grad, near_mixed, near_grad = refs[6:]
    seq = parts[0].shape[0]
    scale = 1.0 / math.sqrt(HEAD)
    for j, part in enumerate(parts):
        branch[j * seq : (j + 1) * seq, :] = part[...]
    mixed_grad[...] = mm_nt(branch[...], out_own[...]).astype(BF16)

    def one(j, carry):
        near = pl.ds(pl.multiple_of(j * seq, seq), seq)
        far = pl.ds(pl.multiple_of(order[j] * seq, seq), seq)
        near_mixed[near, :] = mixed[far, :]
        for h in range(heads):
            at = [(kind * heads + h) * HEAD for kind in range(3)]
            query, key, value = [qkv[far, a : a + HEAD] for a in at]
            grad = mixed_grad[near, h * HEAD : (h + 1) * HEAD]
            probs = head_probs(query, key, scale)
            value_grad = mm_tn(probs.astype(BF16), grad)
            probs_grad = mm_nt(grad, value)
            score_grad = probs * (probs_grad - jnp.sum(probs_grad * probs, axis=-1, keepdims=True))
            score_grad = score_grad.astype(BF16)
            turned = [mm(score_grad, key) * scale, mm_tn(score_grad, query) * scale]
            turned = [g * cos[...] - pltpu.roll(g, HEAD // 2, 1) * sin[...] for g in turned]
            for a, g in zip(at, turned + [value_grad]):
                low = g.astype(BF16)
                near_grad[near, a : a + HEAD] = low
                qkv_grad[far, a : a + HEAD] = low
        return carry

    lax.fori_loop(0, size, one, 0)
    normed_grad[...] = mm_nt(near_grad[...], weight[...]).astype(BF16)
    bias_grad[...] = jnp.sum(near_grad[...].astype(F32), axis=0, keepdims=True)
    out_grad[...] = mm_tn(near_mixed[...], branch[...]).astype(BF16)


def attend_back(order, parts, qkv, mixed, out_own, weight):
    size = len(parts)
    seq, width = parts[0].shape
    wide = weight.shape[1]
    own = wide // 3
    cos, sin = rotary_tables(seq)

    def whole(shape):
        return pl.BlockSpec(shape, lambda i, order: (0, 0))

    inputs = list(parts) + [qkv, mixed, out_own, weight, jnp.asarray(cos), jnp.asarray(sin)]
    shapes = [
        jax.ShapeDtypeStruct((size * seq, width), BF16),
        jax.ShapeDtypeStruct((size * seq, wide), BF16),
        jax.ShapeDtypeStruct((own, width), BF16),
        jax.ShapeDtypeStruct((1, wide), F32),
    ]
    return pl.pallas_call(
        functools.partial(attend_back_kernel, own // HEAD, size),
        grid_spec=pltpu.PrefetchScalarGridSpec(
            num_scalar_prefetch=1,
            grid=(1,),
            in_specs=[whole(a.shape) for a in inputs],
            out_specs=[whole(a.shape) for a in shapes],
            scratch_shapes=[
                pltpu.VMEM((size * seq, width), BF16),
                pltpu.VMEM((size * seq, own), BF16),
                pltpu.VMEM((size * seq, own), BF16),
                pltpu.VMEM((size * seq, wide), BF16),
            ],
        ),
        out_shape=shapes,
        compiler_params=pltpu.CompilerParams(vmem_limit_bytes=60 << 20),
        name="attend_back",
    )(order, *inputs)


def shards(
    tokens,
    lengths,
    routes,
    gate_values,
    cotangent,
    norm1_gain,
    qkv_weight,
    qkv_bias,
    out_weight,
    norm2_gain,
    shared_in,
    shared_out,
    shared_gate,
    expert_in,
    expert_out,
):
    rows, width = tokens.shape
    top = routes.shape[1]
    group = lax.axis_size("expert")
    planes = lax.axis_size("dp")
    devices = group * planes
    both = ("dp", "expert")
    me = lax.axis_index("expert")
    plane = lax.axis_index("dp")
    heads = width // HEAD
    own_heads = heads // group
    shard = qkv_weight.shape[0]
    split = HEAD // shard
    lanes = group // split
    experts = group * expert_in.shape[0]
    valid_total = 23 * rows * devices // 32
    capacity = 5 * valid_total * top // (4 * experts * planes)
    slots = -(-capacity // 16) * 16
    order = plane_order(group, me)
    order_list = jnp.stack(order)
    group_rows = group * rows

    vectors = jnp.concatenate([norm1_gain, norm2_gain, shared_gate, qkv_bias]).astype(F32)
    vector_rows = -(-vectors.shape[0] // 128)
    vectors = jnp.pad(vectors, (0, vector_rows * 128 - vectors.shape[0])).reshape(vector_rows, 128)
    info = jnp.concatenate(
        [
            vectors,
            routes.T.astype(F32),
            gate_values.T,
            jnp.broadcast_to(lengths.astype(F32)[:, None], (1, rows)),
        ],
        axis=0,
    )
    lane, part = me // split, me % split
    out_parts = lax.all_gather(out_weight[None], "dp", axis=0, tiled=True)
    by_head = qkv_weight.reshape(shard, 3, split, own_heads, lanes, HEAD)
    by_head = by_head.transpose(4, 2, 0, 1, 3, 5).reshape(group, shard, 3 * own_heads * HEAD)
    by_head = lax.all_to_all(by_head, "expert", 0, 0, tiled=True)
    by_head, token_source, cot_source = barrier((by_head, tokens, cotangent))
    out_parts, info = barrier((out_parts, info))
    qkv_own = lax.all_gather(by_head, "dp", axis=0, tiled=True).reshape(width, 3 * own_heads * HEAD)

    told = lax.all_to_all(
        jnp.broadcast_to(info[None], (devices,) + info.shape), both, 0, 0, tiled=True
    )
    flat = told[:, :vector_rows].reshape(devices, vector_rows * 128)
    norm1_full = flat[:, :shard].reshape(width)
    norm2_full = flat[:, shard : 2 * shard].reshape(width)
    gate_full = flat[:, 2 * shard : 3 * shard].reshape(width)
    bias_full = flat[:, 3 * shard : 3 * shard + qkv_bias.shape[0]].reshape(
        3, split, own_heads, lanes, HEAD
    )
    rest = told[:, vector_rows:].reshape(planes, group, 2 * top + 1, rows)
    column = lax.dynamic_index_in_dim(rest, me, 1, keepdims=False)
    slot = jnp.arange(rows, dtype=F32)
    all_routes = rest[:, :, :top].astype(jnp.int32)
    all_gates = rest[:, :, top : 2 * top]
    all_valid = slot < rest[:, :, 2 * top]
    column_valid = (slot[None, :] < column[:, 2 * top]).astype(F32).reshape(planes * rows, 1)
    valid_float = (slot < lengths.astype(F32)[0]).astype(F32)[:, None]

    bias_own = lax.dynamic_index_in_dim(bias_full, part, 1, keepdims=False)
    bias_own = lax.dynamic_index_in_dim(bias_own, lane, 2, keepdims=False).reshape(-1)
    pairs = [[k * split + p for p in range(split)] for k in range(lanes)]
    out_seen = gather_second(
        gather_first(out_parts.reshape(split, own_heads, shard, width), group), group
    )
    cot_seen = gather_second(gather_first(cot_source, group), group)
    group_tokens = plane_rows(plane_gather(token_source, group), order)
    group_tokens, unit_in = barrier((group_tokens, shared_in.transpose(1, 2, 0)))
    unit_in = gather_first(unit_in, group)
    qkv_own, column_source = barrier((qkv_own, cotangent))
    column_cot = lax.all_gather(column_source, "dp", axis=0, tiled=True)

    own_width = own_heads * HEAD
    positions = jnp.arange(rows, dtype=jnp.int32)
    places = jnp.arange(group, dtype=jnp.int32)
    normed1, qkv, mixed = attend(group_tokens, norm1_full, qkv_own, bias_own, rows)
    mixed, unit_in, out_seen = barrier((mixed, unit_in, out_seen))
    mixed_parts = gather_first(mixed, group)
    out_whole = plane_place(
        gather_third(out_seen, group),
        order,
        jnp.zeros((lanes, split, own_heads, split, shard, width), BF16),
        lambda whole, block, source: lax.dynamic_update_slice(
            whole, block[None, :, :, None], (source // split, 0, 0, source % split, 0, 0)
        ),
    ).reshape(width, width)

    mixed_parts, column_cot, cot_seen = barrier((mixed_parts, column_cot, cot_seen))
    mixed_parts = gather_third(gather_second(mixed_parts, group), group)
    group_cot = plane_rows(gather_third(cot_seen, group), order)
    mixed_whole = plane_place(
        mixed_parts,
        order,
        jnp.zeros((group_rows, width), BF16),
        lambda whole, block, source: lax.dynamic_update_slice(whole, block, (0, source * own_width)),
    )
    mixed_whole, unit_out = barrier((mixed_whole, shared_out))
    unit_out = gather_first(unit_out, group)
    group_hidden = group_tokens.astype(F32) + mm(mixed_whole, out_whole)
    group_scale2 = norm_scale(group_hidden)
    group_normed = (group_hidden * group_scale2 * norm2_full).astype(BF16)
    hidden = lax.dynamic_slice_in_dim(group_hidden, me * rows, rows, 0)
    scale2 = lax.dynamic_slice_in_dim(group_scale2, me * rows, rows, 0)
    normed2 = lax.dynamic_slice_in_dim(group_normed, me * rows, rows, 0)
    column_normed = lax.all_gather(normed2, "dp", axis=0, tiled=True)

    named = all_routes == me
    taken = jnp.any(named, axis=2) & all_valid
    gate_here = jnp.sum(jnp.where(named, all_gates, 0.0), axis=2)
    before = (positions[:, None] < positions[None, :]).astype(BF16)
    inside = mm(taken.astype(BF16).reshape(devices, rows), before).reshape(planes, group, rows)
    counts = jnp.sum(taken.astype(F32), axis=2)
    ahead = places[None, :] < places[:, None]
    offsets = jnp.sum(jnp.where(ahead[None], counts[:, None, :], 0.0), axis=2)
    all_rank = (inside + offsets[:, :, None]).astype(jnp.int32)
    all_rank = jnp.where(taken & (all_rank < capacity), all_rank, -1)
    rank = lax.dynamic_index_in_dim(all_rank, plane, 0, keepdims=False)
    gate_own = lax.dynamic_index_in_dim(gate_here, plane, 0, keepdims=False)
    slot_ids = jnp.arange(slots, dtype=jnp.int32)[:, None]
    chosen = rank.reshape(1, group_rows) == slot_ids
    pick = chosen.astype(BF16)
    put = (jnp.take(rank, order_list, axis=0).reshape(1, group_rows) == slot_ids).astype(BF16)
    put_near, put_far = put[:, : group_rows // 2], put[:, group_rows // 2 :]
    row_gate = jnp.sum(
        jnp.where(chosen, gate_own.reshape(1, group_rows), 0.0), axis=1, keepdims=True
    )
    weight_in, weight_out = expert_in[0], expert_out[0]
    hidden_units = weight_out.shape[0]
    expert_rows = mm(pick, group_normed).astype(BF16)
    expert_rows, unit_in, unit_out = barrier((expert_rows, unit_in, unit_out))
    unit_in, unit_out = gather_second(unit_in, group), gather_second(unit_out, group)
    cot_rows = mm(pick, group_cot)
    val_grad = (cot_rows * row_gate).astype(BF16)
    expert_pre = mm(expert_rows, weight_in)
    e_gate, e_up = expert_pre[:, :hidden_units], expert_pre[:, hidden_units:]
    expert_act = swiglu_parts(e_gate, e_up)[1].astype(BF16)
    act_grad = mm_nt(val_grad, weight_out)
    part_units = hidden_units // planes
    gated_act = (expert_act.astype(F32) * row_gate).astype(BF16)
    gated_act = gated_act.reshape(slots, planes, part_units).transpose(1, 0, 2)
    gated_act = lax.all_to_all(gated_act, "dp", 0, 0, tiled=True)
    pre_grad = jnp.concatenate(swiglu_back(e_gate, e_up, act_grad), axis=1).astype(BF16)
    in_gate = mm_tn(expert_rows, pre_grad[:, :hidden_units]).astype(BF16)
    in_gate, pre_grad, unit_in, unit_out = barrier((in_gate, pre_grad, unit_in, unit_out))
    unit_in = jnp.concatenate(gather_third(unit_in, group), axis=1)
    unit_out = jnp.concatenate(gather_third(unit_out, group), axis=0)
    in_up = mm_tn(expert_rows, pre_grad[:, hidden_units:]).astype(BF16)
    row_grad = mm_nt(pre_grad, weight_in).astype(BF16)
    expert_val = mm(expert_act, weight_out)
    pair_dot = jnp.sum(cot_rows * expert_val, axis=1, keepdims=True)
    gated_val = (expert_val * row_gate).astype(BF16)
    grad_far = mm_tn(put_far, row_grad).astype(BF16)
    grad_near = mm_tn(put_near, row_grad).astype(BF16)
    routed_grad = plane_sum(grad_near, grad_far, group)
    units = shared_out.shape[0]
    in_gate_grad = lax.psum_scatter(in_gate, "dp", scatter_dimension=0, tiled=True)
    column_normed, in_up = barrier((column_normed, in_up))
    cot_parts, unit_out = barrier((column_cot, unit_out))
    cot_parts = gather_first(cot_parts, group)
    plane_units = group * units
    shared_weight = jax.nn.sigmoid(
        jnp.sum(column_normed.astype(F32) * gate_full, axis=1, keepdims=True)
    )
    unit_flat = unit_in.reshape(2 * plane_units, width)
    shared_pre = mm_nt(column_normed, unit_flat)
    s_gate, s_up = shared_pre[:, :plane_units], shared_pre[:, plane_units:]
    shared_act = swiglu_parts(s_gate, s_up)[1].astype(BF16)
    shared_val = mm(shared_act, unit_out)
    column_grad = column_cot.astype(F32) * column_valid
    shared_val_grad = (column_grad * shared_weight).astype(BF16)
    logit_grad = jnp.sum(column_grad * shared_val, axis=1, keepdims=True)
    logit_grad = logit_grad * shared_weight * (1.0 - shared_weight)
    gate_grad = jnp.sum(logit_grad * column_normed.astype(F32), axis=0)
    shared_act_grad = mm_nt(shared_val_grad, unit_out)
    shared_pre_grad = jnp.concatenate(swiglu_back(s_gate, s_up, shared_act_grad), axis=1)
    shared_pre_grad = shared_pre_grad.astype(BF16)
    shared_pre_grad, cot_parts = barrier((shared_pre_grad, cot_parts))
    cot_parts = gather_second(cot_parts, group)
    normed_term = mm(shared_pre_grad, unit_flat) + logit_grad * gate_full
    normed_term, in_gate_grad, routed_grad, gated_act = barrier(
        (normed_term.astype(BF16), in_gate_grad, routed_grad, gated_act)
    )
    shared_grad = lax.psum_scatter(normed_term, "dp", scatter_dimension=0, tiled=True)
    half_units = plane_units // 2
    unit_grads = []
    for left, right in (
        (shared_act, shared_val_grad),
        (shared_pre_grad[:, :plane_units], column_normed),
        (shared_pre_grad[:, plane_units:], column_normed),
    ):
        far = mm_tn(left[:, half_units:], right).astype(BF16)
        unit_grads.append((mm_tn(left[:, :half_units], right).astype(BF16), far))
    shared_grad, in_up, unit_grads, gated_val, pair_dot, cot_parts = barrier(
        (shared_grad, in_up, unit_grads, gated_val, pair_dot, cot_parts)
    )
    cot_parts = gather_third(cot_parts, group)
    shared_grad = shared_grad.astype(F32)
    in_up_grad = lax.psum_scatter(in_up, "dp", scatter_dimension=0, tiled=True)
    normed2_grad = shared_grad + routed_grad
    norm_term, norm2_part = norm_back(hidden, scale2, norm2_full, normed2_grad)
    hidden_grad = cotangent.astype(F32) * valid_float + norm_term
    branch_parts = gather_first(hidden_grad.astype(BF16), group)
    unit_grads = [sum_first(near, far, group) for near, far in unit_grads]
    branch_parts, unit_grads = barrier((gather_second(branch_parts, group), unit_grads))
    branch_parts = gather_third(branch_parts, group)
    unit_grads = [sum_hop(total, group, second_hop) for total in unit_grads]

    out_own = lax.dynamic_slice_in_dim(out_whole, me * own_width, own_width, 0)
    normed1_grad, qkv_grad, out_own_grad, bias_part = attend_back(
        order_list, branch_parts, qkv, mixed, out_own, qkv_own
    )
    out_own_grad = out_own_grad.reshape(own_heads, split, shard, width).transpose(1, 0, 2, 3)
    out_own_grad = lax.all_to_all(
        out_own_grad, "expert", 0, 0, axis_index_groups=pairs, tiled=True
    ).reshape(planes, shard, width)
    qkv_grad, unit_grads[0] = barrier((qkv_grad, unit_grads[0]))
    qkv_own_grad = mm_tn(normed1, qkv_grad).astype(BF16)

    flat_rows = group * shard * 3 * own_width // width
    shared_part = (shared_weight * shared_val).astype(BF16).reshape(planes, rows, width)
    joined = jnp.concatenate(
        [qkv_own_grad.reshape(planes, flat_rows, width), out_own_grad, shared_part], axis=1
    )
    (
        joined,
        normed1_grad,
        bias_part,
        unit_grads,
        gated_val,
        pair_dot,
        gated_act,
    ) = barrier(
        (
            joined,
            normed1_grad,
            bias_part.reshape(-1),
            unit_grads,
            gated_val,
            pair_dot,
            gated_act,
        )
    )
    joined = lax.psum_scatter(joined, "dp", scatter_dimension=0, tiled=True)[0]
    half_rows = group_rows // 2
    normed1_grad = plane_sum(normed1_grad[:half_rows], normed1_grad[half_rows:], group)
    expert_in_grad = jnp.concatenate([in_gate_grad, in_up_grad], axis=1).astype(F32)
    out_weight_grad = joined[flat_rows : flat_rows + shard]
    shared_sum = joined[flat_rows + shard :].astype(F32)
    qkv_own_grad = joined[:flat_rows]
    qkv_own_grad = lax.all_to_all(
        qkv_own_grad.reshape(group, shard, 3 * own_width), "expert", 0, 0, tiled=True
    )
    qkv_weight_grad = (
        qkv_own_grad.reshape(lanes, split, shard, 3, own_heads, HEAD)
        .transpose(2, 3, 1, 4, 0, 5)
        .reshape(shard, 3 * width)
        .astype(F32)
    )
    own_tokens = tokens.astype(F32)
    token_term, norm1_part = norm_back(own_tokens, norm_scale(own_tokens), norm1_full, normed1_grad)
    tokens_grad = hidden_grad + token_term

    value_far = mm_tn(put_far, gated_val).astype(BF16)
    value_near = mm_tn(put_near, gated_val).astype(BF16)
    routed_sum = plane_sum(value_near, value_far, group)
    pair_dots = jnp.sum(jnp.where(chosen, pair_dot, 0.0), axis=0).reshape(group, rows)
    pair_back = lax.all_to_all(pair_dots, "expert", 0, 0, tiled=True)
    gate_values_grad = jnp.sum(
        jnp.where(routes.T[None] == places[:, None, None], pair_back[:, None, :], 0.0), axis=0
    ).T

    unit_grads, gated_act, expert_in_grad = barrier((unit_grads, gated_act, expert_in_grad))
    all_pick = (all_rank.reshape(planes, 1, group_rows) == slot_ids[None]).astype(BF16)
    token_act = lax.dot_general(
        all_pick, gated_act, (((1,), (1,)), ((0,), (0,))), preferred_element_type=F32
    )
    token_act = token_act.astype(BF16).reshape(planes, group, rows, part_units)
    expert_out_grad = 0.0
    for source, cot_part in zip(order, cot_parts):
        act_part = lax.dynamic_index_in_dim(token_act, source, 1, keepdims=False)
        expert_out_grad = expert_out_grad + mm_tn(
            act_part.reshape(planes * rows, part_units), cot_part
        )

    unit_grads = [sum_hop(total, group, first_hop) for total in unit_grads]
    shared_out_grad, gate_part, up_part = unit_grads
    shared_in_grad = jnp.stack([gate_part, up_part]).transpose(2, 0, 1)

    here = (jnp.arange(split)[:, None] == part) & (jnp.arange(lanes)[None, :] == lane)
    bias_all = jnp.where(
        here[None, :, None, :, None], bias_part.reshape(3, 1, own_heads, 1, HEAD), 0.0
    ).reshape(devices, qkv_bias.shape[0])
    sums = jnp.concatenate(
        [
            norm1_part.reshape(devices, shard),
            norm2_part.reshape(devices, shard),
            gate_grad.reshape(devices, shard),
            bias_all,
        ],
        axis=1,
    )
    sums = jnp.pad(sums, ((0, 0), (0, vector_rows * 128 - sums.shape[1])))
    sums = lax.all_to_all(sums.reshape(devices, vector_rows, 128), both, 0, 0, tiled=True)
    sums, shared_out_grad, shared_in_grad, routed_sum = barrier(
        (sums, shared_out_grad, shared_in_grad, routed_sum)
    )
    sums = jnp.sum(sums, axis=0).reshape(-1)

    output = (valid_float * (hidden + shared_sum + routed_sum)).astype(BF16)
    return (
        output,
        tokens_grad,
        sums[:shard],
        qkv_weight_grad,
        sums[3 * shard : 3 * shard + qkv_bias.shape[0]],
        out_weight_grad.astype(F32),
        sums[shard : 2 * shard],
        shared_in_grad,
        shared_out_grad,
        sums[2 * shard : 3 * shard],
        expert_in_grad[None],
        expert_out_grad.astype(F32)[None],
        gate_values_grad,
    )


def solution(mesh):
    both = ("dp", "expert")
    in_specs = (
        P(both, None),
        P(both),
        P(both, None),
        P(both, None),
        P(both, None),
        P(both),
        P(both, None),
        P(both),
        P(both, None),
        P(both),
        P(None, None, both),
        P(both, None),
        P(both),
        P("expert", None, None),
        P("expert", None, None),
    )
    out_specs = (
        P(both, None),
        P(both, None),
        P(both),
        P(both, None),
        P(both),
        P(both, None),
        P(both),
        P(None, None, both),
        P(both, None),
        P(both),
        P("expert", "dp", None),
        P("expert", "dp", None),
        P(both, None),
    )
    return jax.shard_map(shards, mesh=mesh, in_specs=in_specs, out_specs=out_specs, check_vma=False)
```

```python
import functools
import math

import jax
import jax.numpy as jnp
import numpy as np
from jax import lax
from jax.experimental import pallas as pl
from jax.experimental.pallas import tpu as pltpu
from jax.sharding import PartitionSpec as P

HEAD = 128
NORM_EPS = 1e-06
THETA = 1000000.0
F32 = jnp.float32
barrier = lax.optimization_barrier
BF16 = jnp.bfloat16


def dot(a, b, dims):
    return lax.dot_general(a, b, (dims, ((), ())), preferred_element_type=F32)


def mm(a, b):
    return dot(a, b, ((1,), (0,)))


def mm_nt(a, b):
    return dot(a, b, ((1,), (1,)))


def mm_tn(a, b):
    return dot(a, b, ((0,), (0,)))


def plane_order(size, me):
    if size == 8:
        even, odd = [0, 2, 4, 6, 1, 5, 3, 7], [0, 4, 2, 6, 1, 3, 5, 7]
        first = me % 2 == 0
        return [me ^ (a if a == b else jnp.where(first, a, b)) for a, b in zip(even, odd)]
    return [me ^ m for m in range(size)]


def first_hop(i):
    return i ^ 2 if i % 2 == 0 else i ^ 4


def second_hop(i):
    return i ^ 4 if i % 2 == 0 else i ^ 2


def send(block, size, target):
    return lax.ppermute(block, "expert", [(i, target(i)) for i in range(size)])


def core_swap(i):
    return i ^ 1


def gather_first(block, size):
    if size == 8:
        return [block, send(block, size, first_hop), send(block, size, second_hop)]
    return [block] + [send(block, size, lambda i, m=m: i ^ m) for m in range(1, size)]


def gather_second(parts, size):
    return parts + [send(parts[1], size, second_hop)] if size == 8 else parts


def gather_third(parts, size):
    return parts + [send(part, size, core_swap) for part in parts] if size == 8 else parts


def plane_gather(block, size):
    return gather_third(gather_second(gather_first(block, size), size), size)


def plane_place(parts, order, whole, place):
    for j, part in enumerate(parts):
        whole = place(whole, part, order[j])
    return whole


def plane_rows(parts, order):
    rows = parts[0].shape[0]
    whole = jnp.zeros((len(parts) * rows,) + parts[0].shape[1:], parts[0].dtype)
    return plane_place(
        parts,
        order,
        whole,
        lambda whole, part, source: lax.dynamic_update_slice_in_dim(whole, part, source * rows, 0),
    )


def sum_first(near, far, size):
    if size == 8:
        return near.astype(F32) + send(far.astype(BF16), size, core_swap).astype(F32)
    parts = jnp.concatenate([near.astype(BF16), far.astype(BF16)], axis=0)
    parts = parts.reshape((size, parts.shape[0] // size) + parts.shape[1:])
    total = parts[0].astype(F32)
    for m in range(1, size):
        total = total + send(parts[m], size, lambda i, m=m: i ^ m).astype(F32)
    return total


def sum_hop(near, size, hop):
    if size != 8:
        return near
    half = near.shape[0] // 2
    return near[:half] + send(near[half:].astype(BF16), size, hop).astype(F32)


def plane_sum(near, far, size):
    near = sum_hop(sum_first(near, far, size), size, second_hop)
    return sum_hop(near, size, first_hop)


def norm_scale(rows):
    return lax.rsqrt(jnp.mean(rows * rows, axis=-1, keepdims=True) + NORM_EPS)


def norm_back(rows, scale, gain, grad):
    unit = rows * scale
    weighted = grad * gain
    inner = jnp.mean(weighted * unit, axis=-1, keepdims=True)
    return scale * (weighted - unit * inner), jnp.sum(grad * unit, axis=0)


def swiglu_parts(gate, up):
    sig = jax.nn.sigmoid(gate)
    return sig, gate * sig * up


def swiglu_back(gate, up, grad):
    sig = jax.nn.sigmoid(gate)
    silu = gate * sig
    return grad * up * (sig + silu * (1.0 - sig)), grad * silu


def rotary_tables(row_count):
    half = HEAD // 2
    powers = -(np.arange(half, dtype=np.float32) * np.float32(2.0)) / np.float32(HEAD)
    freqs = np.power(np.float32(THETA), powers).astype(np.float32)
    angles = np.arange(row_count, dtype=np.float32)[:, None] * freqs[None, :]
    cos, sin = np.cos(angles), np.sin(angles)
    return np.concatenate([cos, cos], axis=1), np.concatenate([-sin, sin], axis=1)


def head_probs(query, key, scale):
    scores = mm_nt(query, key) * scale
    shape = scores.shape
    causal = lax.broadcasted_iota(jnp.int32, shape, 0) >= lax.broadcasted_iota(jnp.int32, shape, 1)
    scores = jnp.where(causal, scores, -1e30)
    raised = jnp.exp(scores - jnp.max(scores, axis=-1, keepdims=True))
    return raised / jnp.sum(raised, axis=-1, keepdims=True)


def attend_kernel(
    heads, seq, tokens, gain, weight, bias, cos, sin, normed_out, qkv_out, mixed_out, lin
):
    rows = tokens[...].astype(F32)
    normed_out[...] = (rows * norm_scale(rows) * gain[...]).astype(BF16)
    lin[...] = mm(normed_out[...], weight[...]) + bias[...]
    for s in range(tokens.shape[0] // seq):
        row = slice(s * seq, (s + 1) * seq)
        for h in range(heads):
            low = []
            for kind in range(3):
                at = (kind * heads + h) * HEAD
                part = lin[row, at : at + HEAD]
                if kind < 2:
                    part = part * cos[...] + pltpu.roll(part, HEAD // 2, 1) * sin[...]
                low.append(part.astype(BF16))
                qkv_out[row, at : at + HEAD] = low[-1]
            probs = head_probs(low[0], low[1], 1.0 / math.sqrt(HEAD))
            mixed_out[row, h * HEAD : (h + 1) * HEAD] = mm(probs.astype(BF16), low[2]).astype(BF16)


def attend(tokens, gain, weight, bias, seq):
    total, width = tokens.shape
    wide = weight.shape[1]
    heads = wide // (3 * HEAD)
    rows = 4 * seq
    cos, sin = rotary_tables(seq)

    def whole(shape):
        return pl.BlockSpec(shape, lambda i: (0, 0))

    def block(columns):
        return pl.BlockSpec((rows, columns), lambda i: (i, 0))

    return pl.pallas_call(
        functools.partial(attend_kernel, heads, seq),
        grid=(total // rows,),
        in_specs=[
            block(width),
            whole((1, width)),
            whole((width, wide)),
            whole((1, wide)),
            whole((seq, HEAD)),
            whole((seq, HEAD)),
        ],
        out_specs=[block(width), block(wide), block(heads * HEAD)],
        out_shape=[
            jax.ShapeDtypeStruct((total, width), BF16),
            jax.ShapeDtypeStruct((total, wide), BF16),
            jax.ShapeDtypeStruct((total, heads * HEAD), BF16),
        ],
        scratch_shapes=[pltpu.VMEM((rows, wide), F32)],
        compiler_params=pltpu.CompilerParams(vmem_limit_bytes=48 << 20),
        name="attend",
    )(tokens, gain[None], weight, bias[None], jnp.asarray(cos), jnp.asarray(sin))


def attend_back_kernel(heads, size, order, *refs):
    parts, refs = refs[:size], refs[size:]
    qkv, mixed, out_own, weight, cos, sin = refs[:6]
    normed_grad, qkv_grad, out_grad, bias_grad, branch, mixed_grad, near_mixed, near_grad = refs[6:]
    seq = parts[0].shape[0]
    scale = 1.0 / math.sqrt(HEAD)
    for j, part in enumerate(parts):
        branch[j * seq : (j + 1) * seq, :] = part[...]
    mixed_grad[...] = mm_nt(branch[...], out_own[...]).astype(BF16)

    def one(j, carry):
        near = pl.ds(pl.multiple_of(j * seq, seq), seq)
        far = pl.ds(pl.multiple_of(order[j] * seq, seq), seq)
        near_mixed[near, :] = mixed[far, :]
        for h in range(heads):
            at = [(kind * heads + h) * HEAD for kind in range(3)]
            query, key, value = [qkv[far, a : a + HEAD] for a in at]
            grad = mixed_grad[near, h * HEAD : (h + 1) * HEAD]
            probs = head_probs(query, key, scale)
            value_grad = mm_tn(probs.astype(BF16), grad)
            probs_grad = mm_nt(grad, value)
            score_grad = probs * (probs_grad - jnp.sum(probs_grad * probs, axis=-1, keepdims=True))
            score_grad = score_grad.astype(BF16)
            turned = [mm(score_grad, key) * scale, mm_tn(score_grad, query) * scale]
            turned = [g * cos[...] - pltpu.roll(g, HEAD // 2, 1) * sin[...] for g in turned]
            for a, g in zip(at, turned + [value_grad]):
                low = g.astype(BF16)
                near_grad[near, a : a + HEAD] = low
                qkv_grad[far, a : a + HEAD] = low
        return carry

    lax.fori_loop(0, size, one, 0)
    normed_grad[...] = mm_nt(near_grad[...], weight[...]).astype(BF16)
    bias_grad[...] = jnp.sum(near_grad[...].astype(F32), axis=0, keepdims=True)
    out_grad[...] = mm_tn(near_mixed[...], branch[...]).astype(BF16)


def attend_back(order, parts, qkv, mixed, out_own, weight):
    size = len(parts)
    seq, width = parts[0].shape
    wide = weight.shape[1]
    own = wide // 3
    cos, sin = rotary_tables(seq)

    def whole(shape):
        return pl.BlockSpec(shape, lambda i, order: (0, 0))

    inputs = list(parts) + [qkv, mixed, out_own, weight, jnp.asarray(cos), jnp.asarray(sin)]
    shapes = [
        jax.ShapeDtypeStruct((size * seq, width), BF16),
        jax.ShapeDtypeStruct((size * seq, wide), BF16),
        jax.ShapeDtypeStruct((own, width), BF16),
        jax.ShapeDtypeStruct((1, wide), F32),
    ]
    return pl.pallas_call(
        functools.partial(attend_back_kernel, own // HEAD, size),
        grid_spec=pltpu.PrefetchScalarGridSpec(
            num_scalar_prefetch=1,
            grid=(1,),
            in_specs=[whole(a.shape) for a in inputs],
            out_specs=[whole(a.shape) for a in shapes],
            scratch_shapes=[
                pltpu.VMEM((size * seq, width), BF16),
                pltpu.VMEM((size * seq, own), BF16),
                pltpu.VMEM((size * seq, own), BF16),
                pltpu.VMEM((size * seq, wide), BF16),
            ],
        ),
        out_shape=shapes,
        compiler_params=pltpu.CompilerParams(vmem_limit_bytes=60 << 20),
        name="attend_back",
    )(order, *inputs)


def shards(
    tokens,
    lengths,
    routes,
    gate_values,
    cotangent,
    norm1_gain,
    qkv_weight,
    qkv_bias,
    out_weight,
    norm2_gain,
    shared_in,
    shared_out,
    shared_gate,
    expert_in,
    expert_out,
):
    rows, width = tokens.shape
    top = routes.shape[1]
    group = lax.axis_size("expert")
    planes = lax.axis_size("dp")
    devices = group * planes
    both = ("dp", "expert")
    me = lax.axis_index("expert")
    plane = lax.axis_index("dp")
    heads = width // HEAD
    own_heads = heads // group
    shard = qkv_weight.shape[0]
    split = HEAD // shard
    lanes = group // split
    experts = group * expert_in.shape[0]
    valid_total = 23 * rows * devices // 32
    capacity = 5 * valid_total * top // (4 * experts * planes)
    slots = -(-capacity // 16) * 16
    order = plane_order(group, me)
    order_list = jnp.stack(order)
    group_rows = group * rows

    vectors = jnp.concatenate([norm1_gain, norm2_gain, shared_gate, qkv_bias]).astype(F32)
    vector_rows = -(-vectors.shape[0] // 128)
    vectors = jnp.pad(vectors, (0, vector_rows * 128 - vectors.shape[0])).reshape(vector_rows, 128)
    info = jnp.concatenate(
        [
            vectors,
            routes.T.astype(F32),
            gate_values.T,
            jnp.broadcast_to(lengths.astype(F32)[:, None], (1, rows)),
        ],
        axis=0,
    )
    lane, part = me // split, me % split
    out_parts = lax.all_gather(out_weight[None], "dp", axis=0, tiled=True)
    by_head = qkv_weight.reshape(shard, 3, split, own_heads, lanes, HEAD)
    by_head = by_head.transpose(4, 2, 0, 1, 3, 5).reshape(group, shard, 3 * own_heads * HEAD)
    by_head = lax.all_to_all(by_head, "expert", 0, 0, tiled=True)
    by_head, token_source, cot_source = barrier((by_head, tokens, cotangent))
    out_parts, info = barrier((out_parts, info))
    qkv_own = lax.all_gather(by_head, "dp", axis=0, tiled=True).reshape(width, 3 * own_heads * HEAD)

    told = lax.all_to_all(
        jnp.broadcast_to(info[None], (devices,) + info.shape), both, 0, 0, tiled=True
    )
    flat = told[:, :vector_rows].reshape(devices, vector_rows * 128)
    norm1_full = flat[:, :shard].reshape(width)
    norm2_full = flat[:, shard : 2 * shard].reshape(width)
    gate_full = flat[:, 2 * shard : 3 * shard].reshape(width)
    bias_full = flat[:, 3 * shard : 3 * shard + qkv_bias.shape[0]].reshape(
        3, split, own_heads, lanes, HEAD
    )
    rest = told[:, vector_rows:].reshape(planes, group, 2 * top + 1, rows)
    column = lax.dynamic_index_in_dim(rest, me, 1, keepdims=False)
    slot = jnp.arange(rows, dtype=F32)
    all_routes = rest[:, :, :top].astype(jnp.int32)
    all_gates = rest[:, :, top : 2 * top]
    all_valid = slot < rest[:, :, 2 * top]
    column_valid = (slot[None, :] < column[:, 2 * top]).astype(F32).reshape(planes * rows, 1)
    valid_float = (slot < lengths.astype(F32)[0]).astype(F32)[:, None]

    bias_own = lax.dynamic_index_in_dim(bias_full, part, 1, keepdims=False)
    bias_own = lax.dynamic_index_in_dim(bias_own, lane, 2, keepdims=False).reshape(-1)
    pairs = [[k * split + p for p in range(split)] for k in range(lanes)]
    out_seen = gather_second(
        gather_first(out_parts.reshape(split, own_heads, shard, width), group), group
    )
    cot_seen = gather_second(gather_first(cot_source, group), group)
    group_tokens = plane_rows(plane_gather(token_source, group), order)
    group_tokens, unit_in = barrier((group_tokens, shared_in.transpose(1, 2, 0)))
    unit_in = gather_first(unit_in, group)
    qkv_own, column_source = barrier((qkv_own, cotangent))
    column_cot = lax.all_gather(column_source, "dp", axis=0, tiled=True)

    own_width = own_heads * HEAD
    positions = jnp.arange(rows, dtype=jnp.int32)
    places = jnp.arange(group, dtype=jnp.int32)
    normed1, qkv, mixed = attend(group_tokens, norm1_full, qkv_own, bias_own, rows)
    mixed, unit_in, out_seen = barrier((mixed, unit_in, out_seen))
    mixed_parts = gather_first(mixed, group)
    out_whole = plane_place(
        gather_third(out_seen, group),
        order,
        jnp.zeros((lanes, split, own_heads, split, shard, width), BF16),
        lambda whole, block, source: lax.dynamic_update_slice(
            whole, block[None, :, :, None], (source // split, 0, 0, source % split, 0, 0)
        ),
    ).reshape(width, width)

    mixed_parts, column_cot, cot_seen = barrier((mixed_parts, column_cot, cot_seen))
    mixed_parts = gather_third(gather_second(mixed_parts, group), group)
    group_cot = plane_rows(gather_third(cot_seen, group), order)
    mixed_whole = plane_place(
        mixed_parts,
        order,
        jnp.zeros((group_rows, width), BF16),
        lambda whole, block, source: lax.dynamic_update_slice(whole, block, (0, source * own_width)),
    )
    mixed_whole, unit_out = barrier((mixed_whole, shared_out))
    unit_out = gather_first(unit_out, group)
    group_hidden = group_tokens.astype(F32) + mm(mixed_whole, out_whole)
    group_scale2 = norm_scale(group_hidden)
    group_normed = (group_hidden * group_scale2 * norm2_full).astype(BF16)
    hidden = lax.dynamic_slice_in_dim(group_hidden, me * rows, rows, 0)
    scale2 = lax.dynamic_slice_in_dim(group_scale2, me * rows, rows, 0)
    normed2 = lax.dynamic_slice_in_dim(group_normed, me * rows, rows, 0)
    column_normed = lax.all_gather(normed2, "dp", axis=0, tiled=True)

    named = all_routes == me
    taken = jnp.any(named, axis=2) & all_valid
    gate_here = jnp.sum(jnp.where(named, all_gates, 0.0), axis=2)
    before = (positions[:, None] < positions[None, :]).astype(BF16)
    inside = mm(taken.astype(BF16).reshape(devices, rows), before).reshape(planes, group, rows)
    counts = jnp.sum(taken.astype(F32), axis=2)
    ahead = places[None, :] < places[:, None]
    offsets = jnp.sum(jnp.where(ahead[None], counts[:, None, :], 0.0), axis=2)
    all_rank = (inside + offsets[:, :, None]).astype(jnp.int32)
    all_rank = jnp.where(taken & (all_rank < capacity), all_rank, -1)
    rank = lax.dynamic_index_in_dim(all_rank, plane, 0, keepdims=False)
    gate_own = lax.dynamic_index_in_dim(gate_here, plane, 0, keepdims=False)
    slot_ids = jnp.arange(slots, dtype=jnp.int32)[:, None]
    chosen = rank.reshape(1, group_rows) == slot_ids
    pick = chosen.astype(BF16)
    put = (jnp.take(rank, order_list, axis=0).reshape(1, group_rows) == slot_ids).astype(BF16)
    put_near, put_far = put[:, : group_rows // 2], put[:, group_rows // 2 :]
    row_gate = jnp.sum(
        jnp.where(chosen, gate_own.reshape(1, group_rows), 0.0), axis=1, keepdims=True
    )
    weight_in, weight_out = expert_in[0], expert_out[0]
    hidden_units = weight_out.shape[0]
    expert_rows = mm(pick, group_normed).astype(BF16)
    expert_rows, unit_in, unit_out = barrier((expert_rows, unit_in, unit_out))
    unit_in, unit_out = gather_second(unit_in, group), gather_second(unit_out, group)
    cot_rows = mm(pick, group_cot)
    val_grad = (cot_rows * row_gate).astype(BF16)
    expert_pre = mm(expert_rows, weight_in)
    e_gate, e_up = expert_pre[:, :hidden_units], expert_pre[:, hidden_units:]
    expert_act = swiglu_parts(e_gate, e_up)[1].astype(BF16)
    act_grad = mm_nt(val_grad, weight_out)
    part_units = hidden_units // planes
    gated_act = (expert_act.astype(F32) * row_gate).astype(BF16)
    gated_act = gated_act.reshape(slots, planes, part_units).transpose(1, 0, 2)
    gated_act = lax.all_to_all(gated_act, "dp", 0, 0, tiled=True)
    pre_grad = jnp.concatenate(swiglu_back(e_gate, e_up, act_grad), axis=1).astype(BF16)
    in_gate = mm_tn(expert_rows, pre_grad[:, :hidden_units]).astype(BF16)
    in_gate, pre_grad, unit_in, unit_out = barrier((in_gate, pre_grad, unit_in, unit_out))
    unit_in = jnp.concatenate(gather_third(unit_in, group), axis=1)
    unit_out = jnp.concatenate(gather_third(unit_out, group), axis=0)
    in_up = mm_tn(expert_rows, pre_grad[:, hidden_units:]).astype(BF16)
    row_grad = mm_nt(pre_grad, weight_in).astype(BF16)
    expert_val = mm(expert_act, weight_out)
    pair_dot = jnp.sum(cot_rows * expert_val, axis=1, keepdims=True)
    gated_val = (expert_val * row_gate).astype(BF16)
    grad_far = mm_tn(put_far, row_grad).astype(BF16)
    grad_near = mm_tn(put_near, row_grad).astype(BF16)
    routed_grad = plane_sum(grad_near, grad_far, group)
    units = shared_out.shape[0]
    in_gate_grad = lax.psum_scatter(in_gate, "dp", scatter_dimension=0, tiled=True)
    column_normed, in_up = barrier((column_normed, in_up))
    cot_parts, unit_out = barrier((column_cot, unit_out))
    cot_parts = gather_first(cot_parts, group)
    plane_units = group * units
    shared_weight = jax.nn.sigmoid(
        jnp.sum(column_normed.astype(F32) * gate_full, axis=1, keepdims=True)
    )
    unit_flat = unit_in.reshape(2 * plane_units, width)
    shared_pre = mm_nt(column_normed, unit_flat)
    s_gate, s_up = shared_pre[:, :plane_units], shared_pre[:, plane_units:]
    shared_act = swiglu_parts(s_gate, s_up)[1].astype(BF16)
    shared_val = mm(shared_act, unit_out)
    column_grad = column_cot.astype(F32) * column_valid
    shared_val_grad = (column_grad * shared_weight).astype(BF16)
    logit_grad = jnp.sum(column_grad * shared_val, axis=1, keepdims=True)
    logit_grad = logit_grad * shared_weight * (1.0 - shared_weight)
    gate_grad = jnp.sum(logit_grad * column_normed.astype(F32), axis=0)
    shared_act_grad = mm_nt(shared_val_grad, unit_out)
    shared_pre_grad = jnp.concatenate(swiglu_back(s_gate, s_up, shared_act_grad), axis=1)
    shared_pre_grad = shared_pre_grad.astype(BF16)
    shared_pre_grad, cot_parts = barrier((shared_pre_grad, cot_parts))
    cot_parts = gather_second(cot_parts, group)
    normed_term = mm(shared_pre_grad, unit_flat) + logit_grad * gate_full
    normed_term, in_gate_grad, routed_grad, gated_act = barrier(
        (normed_term.astype(BF16), in_gate_grad, routed_grad, gated_act)
    )
    shared_grad = lax.psum_scatter(normed_term, "dp", scatter_dimension=0, tiled=True)
    half_units = plane_units // 2
    unit_grads = []
    for left, right in (
        (shared_act, shared_val_grad),
        (shared_pre_grad[:, :plane_units], column_normed),
        (shared_pre_grad[:, plane_units:], column_normed),
    ):
        far = mm_tn(left[:, half_units:], right).astype(BF16)
        unit_grads.append((mm_tn(left[:, :half_units], right).astype(BF16), far))
    shared_grad, in_up, unit_grads, gated_val, pair_dot, cot_parts = barrier(
        (shared_grad, in_up, unit_grads, gated_val, pair_dot, cot_parts)
    )
    cot_parts = gather_third(cot_parts, group)
    shared_grad = shared_grad.astype(F32)
    in_up_grad = lax.psum_scatter(in_up, "dp", scatter_dimension=0, tiled=True)
    normed2_grad = shared_grad + routed_grad
    norm_term, norm2_part = norm_back(hidden, scale2, norm2_full, normed2_grad)
    hidden_grad = cotangent.astype(F32) * valid_float + norm_term
    branch_parts = gather_first(hidden_grad.astype(BF16), group)
    unit_grads = [sum_first(near, far, group) for near, far in unit_grads]
    branch_parts, unit_grads = barrier((gather_second(branch_parts, group), unit_grads))
    branch_parts = gather_third(branch_parts, group)
    unit_grads = [sum_hop(total, group, second_hop) for total in unit_grads]

    out_own = lax.dynamic_slice_in_dim(out_whole, me * own_width, own_width, 0)
    normed1_grad, qkv_grad, out_own_grad, bias_part = attend_back(
        order_list, branch_parts, qkv, mixed, out_own, qkv_own
    )
    out_own_grad = out_own_grad.reshape(own_heads, split, shard, width).transpose(1, 0, 2, 3)
    out_own_grad = lax.all_to_all(
        out_own_grad, "expert", 0, 0, axis_index_groups=pairs, tiled=True
    ).reshape(planes, shard, width)
    qkv_own_grad = mm_tn(normed1, qkv_grad).astype(BF16)

    flat_rows = group * shard * 3 * own_width // width
    shared_part = (shared_weight * shared_val).astype(BF16).reshape(planes, rows, width)
    joined = jnp.concatenate(
        [qkv_own_grad.reshape(planes, flat_rows, width), out_own_grad, shared_part], axis=1
    )
    (
        joined,
        normed1_grad,
        bias_part,
        unit_grads,
        gated_val,
        pair_dot,
        gated_act,
    ) = barrier(
        (
            joined,
            normed1_grad,
            bias_part.reshape(-1),
            unit_grads,
            gated_val,
            pair_dot,
            gated_act,
        )
    )
    joined = lax.psum_scatter(joined, "dp", scatter_dimension=0, tiled=True)[0]
    half_rows = group_rows // 2
    normed1_grad = plane_sum(normed1_grad[:half_rows], normed1_grad[half_rows:], group)
    expert_in_grad = jnp.concatenate([in_gate_grad, in_up_grad], axis=1).astype(F32)
    out_weight_grad = joined[flat_rows : flat_rows + shard]
    shared_sum = joined[flat_rows + shard :].astype(F32)
    qkv_own_grad = joined[:flat_rows]
    qkv_own_grad = lax.all_to_all(
        qkv_own_grad.reshape(group, shard, 3 * own_width), "expert", 0, 0, tiled=True
    )
    qkv_weight_grad = (
        qkv_own_grad.reshape(lanes, split, shard, 3, own_heads, HEAD)
        .transpose(2, 3, 1, 4, 0, 5)
        .reshape(shard, 3 * width)
        .astype(F32)
    )
    own_tokens = tokens.astype(F32)
    token_term, norm1_part = norm_back(own_tokens, norm_scale(own_tokens), norm1_full, normed1_grad)
    tokens_grad = hidden_grad + token_term

    value_far = mm_tn(put_far, gated_val).astype(BF16)
    value_near = mm_tn(put_near, gated_val).astype(BF16)
    routed_sum = plane_sum(value_near, value_far, group)
    pair_dots = jnp.sum(jnp.where(chosen, pair_dot, 0.0), axis=0).reshape(group, rows)
    pair_back = lax.all_to_all(pair_dots, "expert", 0, 0, tiled=True)
    gate_values_grad = jnp.sum(
        jnp.where(routes.T[None] == places[:, None, None], pair_back[:, None, :], 0.0), axis=0
    ).T

    unit_grads, gated_act, expert_in_grad = barrier((unit_grads, gated_act, expert_in_grad))
    all_pick = (all_rank.reshape(planes, 1, group_rows) == slot_ids[None]).astype(BF16)
    token_act = lax.dot_general(
        all_pick, gated_act, (((1,), (1,)), ((0,), (0,))), preferred_element_type=F32
    )
    token_act = token_act.astype(BF16).reshape(planes, group, rows, part_units)
    expert_out_grad = 0.0
    for source, cot_part in zip(order, cot_parts):
        act_part = lax.dynamic_index_in_dim(token_act, source, 1, keepdims=False)
        expert_out_grad = expert_out_grad + mm_tn(
            act_part.reshape(planes * rows, part_units), cot_part
        )

    unit_grads = [sum_hop(total, group, first_hop) for total in unit_grads]
    shared_out_grad, gate_part, up_part = unit_grads
    shared_in_grad = jnp.stack([gate_part, up_part]).transpose(2, 0, 1)

    here = (jnp.arange(split)[:, None] == part) & (jnp.arange(lanes)[None, :] == lane)
    bias_all = jnp.where(
        here[None, :, None, :, None], bias_part.reshape(3, 1, own_heads, 1, HEAD), 0.0
    ).reshape(devices, qkv_bias.shape[0])
    sums = jnp.concatenate(
        [
            norm1_part.reshape(devices, shard),
            norm2_part.reshape(devices, shard),
            gate_grad.reshape(devices, shard),
            bias_all,
        ],
        axis=1,
    )
    sums = jnp.pad(sums, ((0, 0), (0, vector_rows * 128 - sums.shape[1])))
    sums = lax.all_to_all(sums.reshape(devices, vector_rows, 128), both, 0, 0, tiled=True)
    sums, shared_out_grad, shared_in_grad, routed_sum = barrier(
        (sums, shared_out_grad, shared_in_grad, routed_sum)
    )
    sums = jnp.sum(sums, axis=0).reshape(-1)

    output = (valid_float * (hidden + shared_sum + routed_sum)).astype(BF16)
    return (
        output,
        tokens_grad,
        sums[:shard],
        qkv_weight_grad,
        sums[3 * shard : 3 * shard + qkv_bias.shape[0]],
        out_weight_grad.astype(F32),
        sums[shard : 2 * shard],
        shared_in_grad,
        shared_out_grad,
        sums[2 * shard : 3 * shard],
        expert_in_grad[None],
        expert_out_grad.astype(F32)[None],
        gate_values_grad,
    )


def solution(mesh):
    both = ("dp", "expert")
    in_specs = (
        P(both, None),
        P(both),
        P(both, None),
        P(both, None),
        P(both, None),
        P(both),
        P(both, None),
        P(both),
        P(both, None),
        P(both),
        P(None, None, both),
        P(both, None),
        P(both),
        P("expert", None, None),
        P("expert", None, None),
    )
    out_specs = (
        P(both, None),
        P(both, None),
        P(both),
        P(both, None),
        P(both),
        P(both, None),
        P(both),
        P(None, None, both),
        P(both, None),
        P(both),
        P("expert", "dp", None),
        P("expert", "dp", None),
        P(both, None),
    )
    return jax.shard_map(shards, mesh=mesh, in_specs=in_specs, out_specs=out_specs, check_vma=False)
```
